32 devices in a mesh: groups: 2 (over y), seq: 8 (over z, x), heads: 2 (over core).
Axes of the slice: x: 2, y: 2, z: 4, core: 2. Of those that a mesh axis runs over, the one named last changes fastest.
Arguments:
- queries: bfloat16 [8192, 16, 128], P(('groups', 'seq'), 'heads'), parts along dimension 0, may hold values from -128 to 128
- keys: bfloat16 [8192, 16, 128], P(('groups', 'seq'), 'heads'), parts along dimension 0, may hold values from -128 to 128
- values: bfloat16 [8192, 16, 128], P(('groups', 'seq'), 'heads'), parts along dimension 0, may hold values from -6 to 6
Outputs:
- attended: bfloat16 [8192, 16, 128], P(('groups', 'seq'), 'heads'), parts along dimension 0
The draws below stay inside these ranges and needn't reach their ends.
There are 2 independent parts, one for each index of `groups`. The reference program is written for one: setup_inputs(seed, part) draws one part's arguments, and reference() takes and returns one part's arrays. A program takes and returns all parts, laid end to end along the dimension named above; each array names one. Nothing has to cross between parts.
All inputs are finite; a program needn't handle non-finite values.
Results may differ from the reference program's by a relative error of at most 0.0055.
Values may be sent and summed in bfloat16 or wider, within the bound.
A program may use at most 128 MiB of HBM per device.

```python
import math
import jax
import jax.numpy as jnp
from jax import lax

HEADS = 16
HD = 128
BLOCK = 64
LENGTH = 4096


def paired_fields(key):
    shape = (LENGTH, HEADS, HD)
    queries = jnp.clip(jax.random.normal(jax.random.fold_in(key, 101), shape, jnp.float32), -5.0, 5.0)
    keys = jnp.clip(jax.random.normal(jax.random.fold_in(key, 102), shape, jnp.float32), -5.0, 5.0)
    return (queries, keys)


def draw_queries(key, part):
    return paired_fields(key)[0].astype(jnp.bfloat16)


def draw_keys(key, part):
    return paired_fields(key)[1].astype(jnp.bfloat16)


def block_scale(own_key, extent, shards, smallest, largest):
    factor_of, own = 1.0, jax.random.fold_in(own_key, 6)
    for axis_at, parts in shards:
        draws = jnp.exp(jax.random.uniform(jax.random.fold_in(own, axis_at), (parts,), jnp.float32, smallest / len(shards), largest / len(shards)))
        factor_of = factor_of * jnp.repeat(draws, extent[axis_at] // parts).reshape([-1 if axis == axis_at else 1 for axis in range(len(extent))])
    return factor_of


def bell_draw(stream_key, extent, scale, bound, pieces=(), kind=jnp.bfloat16):
    result = scale * jax.random.normal(stream_key, extent, jnp.float32)
    if pieces:
        result = result * block_scale(stream_key, extent, pieces, -0.22, 0.18)
    return jnp.clip(result, -bound, bound).astype(kind)


def setup_inputs(seed: int = 0, part: int = 0) -> dict:
    key_of = jax.random.split(jax.random.key(seed), 4)
    part_splits = jax.random.split(jax.random.fold_in(key_of[3], part), 4)
    return {
        "queries": draw_queries(jax.random.fold_in(jax.random.fold_in(key_of[3], part), 71), part),
        "keys": draw_keys(jax.random.fold_in(jax.random.fold_in(key_of[3], part), 71), part),
        "values": bell_draw(part_splits[2], (LENGTH, HEADS, HD), 1.0, 6.0, ((0, 8), (1, 2))),
    }


neg_big = -1e+30
log_two = math.log(2.0)

def pool_rows(block, factor):
    count = block.shape[0] // factor
    grouped = block.astype(jnp.float32).reshape(count, factor, block.shape[1], block.shape[2])
    return lax.optimization_barrier(jnp.mean(grouped, axis=1)).astype(jnp.bfloat16)

def level_scores(query_block, key_rows, valid, bias):
    scores = jnp.einsum('qhd,khd->hqk', query_block.astype(jnp.float32), key_rows.astype(jnp.float32))
    scores = scores / math.sqrt(query_block.shape[2]) + bias
    return jnp.where(valid[None], scores, neg_big)

def reference(queries, keys, values):
    length, heads, width = queries.shape
    quad = 4 * BLOCK
    padding = jnp.zeros((BLOCK, heads, width), jnp.bfloat16)
    pooled_k = [pool_rows(keys, 2 ** level) for level in (1, 2, 3)]
    pooled_v = [pool_rows(values, 2 ** level) for level in (1, 2, 3)]
    ext0_k = jnp.concatenate([padding, keys], 0)
    ext0_v = jnp.concatenate([padding, values], 0)
    ext1_k = jnp.concatenate([padding, pooled_k[0]], 0)
    ext1_v = jnp.concatenate([padding, pooled_v[0]], 0)
    ext2_k = jnp.concatenate([padding, pooled_k[1]], 0)
    ext2_v = jnp.concatenate([padding, pooled_v[1]], 0)
    coarse_rows = jnp.arange(length // 8, dtype=jnp.int32)

    def one_block(blk):
        start = (blk * quad).astype(jnp.int32)
        posit = start + jnp.arange(quad, dtype=jnp.int32)
        bound0 = (posit // BLOCK - 1) * BLOCK
        bound1 = (posit // (2 * BLOCK) - 1) * 2 * BLOCK
        bound2 = (posit // quad - 1) * quad
        query_block = lax.dynamic_slice_in_dim(queries, start, quad, 0)
        tokens0 = start - BLOCK + jnp.arange(quad + BLOCK, dtype=jnp.int32)
        rows1 = start // 2 - BLOCK + jnp.arange(quad // 2 + BLOCK, dtype=jnp.int32)
        rows2 = start // 4 - BLOCK + jnp.arange(quad // 4 + BLOCK, dtype=jnp.int32)
        key0 = lax.dynamic_slice_in_dim(ext0_k, start, quad + BLOCK, 0)
        val0 = lax.dynamic_slice_in_dim(ext0_v, start, quad + BLOCK, 0)
        key1 = lax.dynamic_slice_in_dim(ext1_k, (start // 2).astype(jnp.int32), quad // 2 + BLOCK, 0)
        val1 = lax.dynamic_slice_in_dim(ext1_v, (start // 2).astype(jnp.int32), quad // 2 + BLOCK, 0)
        key2 = lax.dynamic_slice_in_dim(ext2_k, (start // 4).astype(jnp.int32), quad // 4 + BLOCK, 0)
        val2 = lax.dynamic_slice_in_dim(ext2_v, (start // 4).astype(jnp.int32), quad // 4 + BLOCK, 0)
        valid0 = (tokens0 >= 0)[None] & (tokens0[None] >= bound0[:, None]) & (tokens0[None] <= posit[:, None])
        valid1 = (rows1 >= 0)[None] & (2 * rows1[None] >= bound1[:, None]) & (2 * rows1[None] + 2 <= bound0[:, None])
        valid2 = (rows2 >= 0)[None] & (4 * rows2[None] >= bound2[:, None]) & (4 * rows2[None] + 4 <= bound1[:, None])
        valid3 = 8 * coarse_rows[None] + 8 <= bound2[:, None]
        scores = jnp.concatenate([level_scores(query_block, key0, valid0, 0.0), level_scores(query_block, key1, valid1, log_two), level_scores(query_block, key2, valid2, 2.0 * log_two), level_scores(query_block, pooled_k[2], valid3, 3.0 * log_two)], axis=2)
        value_rows = jnp.concatenate([val0, val1, val2, pooled_v[2]], 0)
        top = lax.optimization_barrier(jnp.max(scores, axis=2, keepdims=True))
        weights = jnp.exp(scores - top)
        total = lax.optimization_barrier(jnp.sum(weights, axis=2))
        rounded = weights.astype(jnp.bfloat16)
        summed = jnp.einsum('hqk,khd->hqd', rounded.astype(jnp.float32), value_rows.astype(jnp.float32))
        return (summed / total[..., None]).transpose(1, 0, 2).astype(jnp.bfloat16)
    blocks = lax.map(one_block, jnp.arange(length // quad, dtype=jnp.int32))
    return blocks.reshape(length, heads, width)
```

```python
import functools
import math

import jax
import jax.numpy as jnp
from jax import lax
from jax.experimental import pallas as pl
from jax.experimental.pallas import tpu as pltpu
from jax.sharding import PartitionSpec as P

BLOCK = 64
QUAD = 4 * BLOCK
HALF = 2 * BLOCK
NEAR = 6 * BLOCK
NEG = -1e30
F32 = jnp.float32
BF16 = jnp.bfloat16


def to_heads(values, scratch, heads):
    count, _, width = values.shape
    scratch[pl.ds(0, count * heads), :] = values.reshape(count * heads, width)
    return [scratch[pl.ds(h, count, stride=heads), :].astype(BF16) for h in range(heads)]


def halved(values):
    count, heads, width = values.shape
    pairs = values.reshape(count // 2, 2, heads, width)
    return pairs[:, 0] + pairs[:, 1]


def across(column, count):
    width = column.shape[1]
    return jnp.concatenate([column] * (count // width), 1) if count > width else column


def with_ones(values):
    return jnp.concatenate([values, jnp.ones_like(values)], 1)


def kernel(size, q_ref, k_ref, v_ref, o_ref,
           far, tail, thru, sendp, eq, e0, e1, e2, ex, fk,
           bias, acc, top, total, tmp, otmp,
           recv, up_send, side_send, t_send, t_recv, r_send, r_recv):
    rows, heads, width = q_ref.shape
    own = rows // 8
    blocks = rows // BLOCK
    gain = math.log2(math.e) / math.sqrt(width)
    me = lax.axis_index("seq")
    col = lax.rem(me, 2)
    lev = me // 2
    levels = size // 2
    together = 2 - heads % 2
    climbs = lev < levels - 1
    pair = me + 1 - 2 * col
    up = jnp.minimum(me + 2, size - 1)
    sources = (k_ref, v_ref)

    def remote(src, dst, send, got, target):
        return pltpu.make_async_remote_copy(
            src_ref=src, dst_ref=dst, send_sem=send, recv_sem=got,
            device_id={"seq": target}, device_id_type=pl.DeviceIdType.MESH)

    def up_copy(kv, b):
        return remote(far.at[kv, b], far.at[kv, b], up_send.at[kv, b], recv.at[kv, b], up)

    def side_copy(kv, b):
        return remote(far.at[kv, b], far.at[kv, b], side_send.at[kv, b], recv.at[kv, b], pair)

    def tail_source(kv, part):
        return sources[kv].at[pl.ds(rows - BLOCK, BLOCK)] if part == 0 else sendp.at[kv]

    def tail_copy(kv, part):
        return remote(tail_source(kv, part), tail.at[kv, part], t_send.at[kv, part], t_recv.at[kv, part], pair)

    def thru_copy(kv, part):
        return remote(tail_source(kv, part), thru.at[kv, part], t_send.at[kv, part], r_recv.at[kv, part], pair)

    def relay_copy(kv, part):
        return remote(thru.at[kv, part], tail.at[kv, part], r_send.at[kv, part], t_recv.at[kv, part], up)

    barrier = pltpu.get_barrier_semaphore()
    for step in (-2, 2):
        @pl.when((me + step >= 0) & (me + step < size))
        def _():
            pl.semaphore_signal(barrier, inc=1, device_id={"seq": me + step},
                                device_id_type=pl.DeviceIdType.MESH)
    pl.semaphore_signal(barrier, inc=1, device_id={"seq": pair}, device_id_type=pl.DeviceIdType.MESH)

    def split(kv, c):
        x = sources[kv][pl.ds(c * BLOCK, BLOCK)].astype(F32)
        two = halved(x)
        four = halved(two)
        eight = halved(four)
        far[kv, me, pl.ds(c * 8, 8)] = (eight * 0.125).astype(BF16)
        if c == blocks - 2:
            sendp[kv, pl.ds(0, 32)] = (two * 0.5).astype(BF16)
        if blocks - 4 <= c < blocks - 2:
            sendp[kv, pl.ds(32 + 16 * (c - blocks + 4), 16)] = (four * 0.25).astype(BF16)

    def spread(kv, c):
        x = sources[kv][pl.ds(c * BLOCK, BLOCK)].astype(F32)
        for h, part in enumerate(to_heads(x, tmp, heads)):
            e0[kv, h, pl.ds(BLOCK + c * BLOCK, BLOCK), :] = part
        if c < blocks - 2:
            two = halved(x)
            for h, part in enumerate(to_heads(two * 0.5, tmp, heads)):
                e1[kv, h, pl.ds(BLOCK + c * 32, 32), :] = part
            if c < blocks - 4:
                four = halved(two)
                for h, part in enumerate(to_heads(four * 0.25, tmp, heads)):
                    e2[kv, h, pl.ds(BLOCK + c * 16, 16), :] = part

    for kv in (1, 0):
        for c in range(blocks):
            split(kv, c)

    pl.semaphore_wait(barrier, 1 + jnp.where(lev > 0, 1, 0) + jnp.where(climbs, 1, 0))

    @pl.when(col == 0)
    def _():
        side_copy(1, me).start()
        side_copy(0, me).start()

        @pl.when(climbs)
        def _():
            up_copy(0, me).start()
        for kv in range(2):
            for part in range(2):
                tail_copy(kv, part).start()

    @pl.when((col == 1) & climbs)
    def _():
        up_copy(0, me).start()
        up_copy(1, me).start()
        for kv in range(2):
            for part in range(2):
                thru_copy(kv, part).start()

    for kv in range(2):
        for c in range(blocks):
            spread(kv, c)
    for c in range(blocks):
        x = q_ref[pl.ds(c * BLOCK, BLOCK)].astype(F32)
        for h, part in enumerate(to_heads(x, tmp, heads)):
            eq[h, pl.ds(c * BLOCK, BLOCK), :] = part

    i = lax.broadcasted_iota(jnp.int32, (HALF, NEAR), 0)
    j = lax.broadcasted_iota(jnp.int32, (HALF, NEAR), 1)
    is0 = j < 192
    is2 = j >= 256
    is3 = j >= 320
    level = jnp.where(is0, 0.0, jnp.where(is3, 3.0, jnp.where(is2, 2.0, 1.0)))
    ok01 = jnp.where(is0, jnp.where((j <= i + BLOCK) & ((j >= BLOCK) | (i < BLOCK)), 1, 0),
                     jnp.where((j < 224) | (i >= BLOCK), 1, 0))
    for qd in range(rows // QUAD):
        ok3 = jnp.where((col == 1) & ((j < 320 + own // 2) | (qd > 0)), 1, 0)
        for hf in range(2):
            ok = jnp.where(is2, jnp.where((j < 288) | (hf == 1), 1, 0), ok01)
            if qd == 0:
                real = (j >= BLOCK) & (j < 192) if hf == 0 else j < 256
                ok = jnp.where(real | (me > 0), ok, 0)
            ok = jnp.where(is3, ok3, ok)
            bias[2 * qd + hf] = jnp.where(ok > 0, level, NEG)

    def near(qd, first, count):
        def body(g, _):
            for part in range(2 * together):
                h, hf = g * together + part // 2, part % 2
                at = qd * QUAD + hf * HALF
                q = eq[h, pl.ds(at, HALF), :]
                kk, vv = (jnp.concatenate([
                    e0[kv, h, pl.ds(at, 192), :],
                    e1[kv, h, pl.ds(at // 2, BLOCK), :],
                    e2[kv, h, pl.ds(qd * BLOCK, BLOCK), :],
                    ex[kv, h]], 0) for kv in range(2))
                s = lax.dot_general(q, kk, (((1,), (1,)), ((), ())), preferred_element_type=F32)
                s = s * gain + bias[2 * qd + hf]
                m = jnp.broadcast_to(jnp.max(s, axis=1, keepdims=True), (HALF, width))
                w = jnp.exp2(s - across(m, NEAR)).astype(BF16)
                both = jnp.dot(w, with_ones(vv), preferred_element_type=F32)
                top[h, pl.ds(at, HALF), :] = m
                acc[h, pl.ds(at, HALF), :] = both[:, :width]
                total[h, pl.ds(at, HALF), :] = both[:, width:]
            return 0
        lax.fori_loop(first, first + count, body, 0)

    def extra():
        @pl.when(col == 1)
        def _():
            side_copy(0, me - 1).wait_recv()
            for kv in range(2):
                for h, part in enumerate(to_heads(far[kv, me - 1].astype(F32), tmp, heads)):
                    ex[kv, h] = part

        @pl.when(col == 0)
        def _():
            ex[...] = jnp.zeros_like(ex)

    def previous():
        @pl.when(me == 0)
        def _():
            for kv in range(2):
                for h in range(heads):
                    for e in (e0, e1, e2):
                        e[kv, h, pl.ds(0, BLOCK), :] = jnp.zeros((BLOCK, width), BF16)

        @pl.when(me > 0)
        def _():
            for kv in range(2):
                for part in range(2):
                    tail_copy(kv, part).wait_recv()
                x = tail[kv, 0].astype(F32)
                two = halved(x)
                four = halved(two)
                y = tail[kv, 1].astype(F32)
                late = halved(y[:32])
                for h, part in enumerate(to_heads(x, tmp, heads)):
                    e0[kv, h, pl.ds(0, BLOCK), :] = part
                for h, part in enumerate(to_heads(two * 0.5, tmp, heads)):
                    e1[kv, h, pl.ds(32, 32), :] = part
                for h, part in enumerate(to_heads(four * 0.25, tmp, heads)):
                    e2[kv, h, pl.ds(48, 16), :] = part
                for h, part in enumerate(to_heads(late * 0.5, tmp, heads)):
                    e2[kv, h, pl.ds(32, 16), :] = part
                for h, part in enumerate(to_heads(y, tmp, heads)):
                    e1[kv, h, pl.ds(0, 32), :] = part[:32]
                    e2[kv, h, pl.ds(0, 32), :] = part[32:]

    def distant(r):
        odd = me - 2 * r + 1 - col
        even = me - 2 * r - col

        @pl.when(col == 1)
        def _():
            side_copy(0, even).wait_recv()

        @pl.when(col == 0)
        def _():
            side_copy(0, odd).wait_recv()
            side_copy(1, odd).wait_recv()
        for kv in range(2):
            for n, b in enumerate((odd, even)):
                for h, part in enumerate(to_heads(far[kv, b].astype(F32), tmp, heads)):
                    fk[kv, h, pl.ds(n * own, own), :] = part
        place = lax.broadcasted_iota(jnp.int32, (1, 2 * own), 1)
        hide = jnp.where((col == 0) & (r == 1) & (place >= own // 2) & (place < own), NEG, 0.0)

        def body(h, _):
            for qd in range(rows // QUAD):
                for hf in range(2):
                    at = qd * QUAD + hf * HALF
                    m = top[h, pl.ds(at, HALF), :]
                    s = lax.dot_general(eq[h, pl.ds(at, HALF), :], fk[0, h],
                                        (((1,), (1,)), ((), ())), preferred_element_type=F32)
                    if qd == 0:
                        s = s + hide
                    peak = jnp.max(s, axis=1, keepdims=True) * gain + 3.0
                    fresh = jnp.maximum(m, peak)
                    fade = jnp.exp2(m - fresh)
                    w = jnp.exp2(s * gain - across(fresh - 3.0, 2 * own)).astype(BF16)
                    both = jnp.dot(w, with_ones(fk[1, h]), preferred_element_type=F32)
                    top[h, pl.ds(at, HALF), :] = fresh
                    acc[h, pl.ds(at, HALF), :] = acc[h, pl.ds(at, HALF), :] * fade + both[:, :width]
                    total[h, pl.ds(at, HALF), :] = (
                        total[h, pl.ds(at, HALF), :] * fade + both[:, width:])
            return 0

        lax.fori_loop(0, heads, body, 0)

    groups = heads // together
    early = (groups + 1) // 2

    def turn(n, _):
        r = (n - 1) // 3 + 1
        part = lax.rem(n - 1, 3)

        @pl.when((col == 1) & (n == 1))
        def _():
            side_copy(1, me - 1).wait_recv()

            @pl.when(climbs)
            def _():
                up_copy(1, me - 1).start()

        @pl.when((col == 1) & (r <= lev))
        def _():
            kv = jnp.minimum(part, 1)
            b = me - 2 * r - jnp.where(part == 2, 1, 0)
            up_copy(kv, b).wait_recv()

            @pl.when(climbs)
            def _():
                up_copy(kv, b).start()

            @pl.when((part < 2) | (r == 1))
            def _():
                side_copy(kv, b).start()

        @pl.when((col == 0) & (n <= lev))
        def _():
            b = me - 2 * n
            up_copy(0, b).wait_recv()
            side_copy(0, b).start()

            @pl.when(climbs)
            def _():
                up_copy(0, b).start()

        @pl.when((col == 0) & climbs & (n <= 4))
        def _():
            kv, part = (n - 1) // 2, lax.rem(n - 1, 2)
            remote(thru.at[kv, part], thru.at[kv, part], r_send.at[kv, part], r_recv.at[kv, part], pair).wait_recv()
            relay_copy(kv, part).start()

        @pl.when((col == 0) & (n > 4) & (n - 4 <= lev))
        def _():
            b = me - 2 * (n - 4)
            up_copy(1, b).wait_recv()

            @pl.when(climbs)
            def _():
                up_copy(1, b).start()

        @pl.when(n == 2)
        def _():
            extra()

        @pl.when((n == 2) | (n == 3))
        def _():
            for qd in range(1, rows // QUAD):
                near(qd, (n - 2) * early, jnp.where(n == 2, early, groups - early))

        @pl.when(n == 6)
        def _():
            previous()
            near(0, 0, groups)

        gone = jnp.where(n <= 9, n - 6, n // 3)

        @pl.when((gone >= 1) & (gone <= lev) & ((n <= 9) | (lax.rem(n, 3) == 0)))
        def _():
            distant(gone)
        return 0

    lax.fori_loop(1, jnp.maximum(6 + lev, 3 * lev) + 1, turn, 0)

    for c in range(rows // HALF):
        for h in range(heads):
            otmp[pl.ds(h, HALF, stride=heads), :] = (
                acc[h, pl.ds(c * HALF, HALF), :] / total[h, pl.ds(c * HALF, HALF), :])
        o_ref[pl.ds(c * HALF, HALF)] = otmp[...].reshape(HALF, heads, width).astype(BF16)

    @pl.when(col == 0)
    def _():
        side_copy(1, me).wait_send()
        side_copy(0, me).wait_send()
        for kv in range(2):
            for part in range(2):
                tail_copy(kv, part).wait_send()

        @pl.when(climbs)
        def _():
            up_copy(0, me).wait_send()
            for kv in range(2):
                for part in range(2):
                    relay_copy(kv, part).wait_send()

    @pl.when((col == 1) & climbs)
    def _():
        up_copy(0, me).wait_send()
        up_copy(1, me).wait_send()
        up_copy(1, me - 1).wait_send()
        for kv in range(2):
            for part in range(2):
                thru_copy(kv, part).wait_send()

    def sent(r, _):
        b = me - 2 * r
        side_copy(0, b).wait_send()

        @pl.when(climbs)
        def _():
            up_copy(0, b).wait_send()
            up_copy(1, b).wait_send()

        @pl.when(col == 1)
        def _():
            side_copy(1, b).wait_send()

            @pl.when(climbs)
            def _():
                up_copy(1, b - 1).wait_send()

            @pl.when(r == 1)
            def _():
                side_copy(1, b - 1).wait_send()
        return 0

    lax.fori_loop(1, lev + 1, sent, 0)


def shards(size, queries, keys, values):
    rows, heads, width = queries.shape
    own = rows // 8
    vmem = pl.BlockSpec(memory_space=pltpu.VMEM)
    return pl.pallas_call(
        functools.partial(kernel, size),
        out_shape=jax.ShapeDtypeStruct((rows, heads, width), BF16),
        in_specs=[vmem] * 3,
        out_specs=vmem,
        scratch_shapes=[
            pltpu.VMEM((2, size, own, heads, width), BF16),
            pltpu.VMEM((2, 2, BLOCK, heads, width), BF16),
            pltpu.VMEM((2, 2, BLOCK, heads, width), BF16),
            pltpu.VMEM((2, BLOCK, heads, width), BF16),
            pltpu.VMEM((heads, rows, width), BF16),
            pltpu.VMEM((2, heads, rows + BLOCK, width), BF16),
            pltpu.VMEM((2, heads, rows // 2, width), BF16),
            pltpu.VMEM((2, heads, rows // 4, width), BF16),
            pltpu.VMEM((2, heads, own, width), BF16),
            pltpu.VMEM((2, heads, 2 * own, width), BF16),
            pltpu.VMEM((rows // HALF, HALF, NEAR), F32),
            pltpu.VMEM((heads, rows, width), F32),
            pltpu.VMEM((heads, rows, width), F32),
            pltpu.VMEM((heads, rows, width), F32),
            pltpu.VMEM((80 * heads, width), F32),
            pltpu.VMEM((HALF * heads, width), F32),
            pltpu.SemaphoreType.DMA((2, size)),
            pltpu.SemaphoreType.DMA((2, size)),
            pltpu.SemaphoreType.DMA((2, size)),
            pltpu.SemaphoreType.DMA((2, 2)),
            pltpu.SemaphoreType.DMA((2, 2)),
            pltpu.SemaphoreType.DMA((2, 2)),
            pltpu.SemaphoreType.DMA((2, 2)),
        ],
        compiler_params=pltpu.CompilerParams(
            collective_id=0, has_side_effects=True, vmem_limit_bytes=60 * 2**20),
    )(queries, keys, values)


def solution(mesh):
    spec = P(("groups", "seq"), "heads", None)
    return jax.shard_map(
        functools.partial(shards, mesh.shape["seq"]),
        mesh=mesh, in_specs=(spec,) * 3, out_specs=spec, check_vma=False)
```

```python
import functools
import math

import jax
import jax.numpy as jnp
from jax import lax
from jax.experimental import pallas as pl
from jax.experimental.pallas import tpu as pltpu
from jax.sharding import PartitionSpec as P

BLOCK = 64
QUAD = 4 * BLOCK
HALF = 2 * BLOCK
NEAR = 6 * BLOCK
NEG = -1e30
F32 = jnp.float32
BF16 = jnp.bfloat16


def to_heads(values, scratch, heads):
    count, _, width = values.shape
    scratch[pl.ds(0, count * heads), :] = values.reshape(count * heads, width)
    return [scratch[pl.ds(h, count, stride=heads), :].astype(BF16) for h in range(heads)]


def halved(values):
    count, heads, width = values.shape
    pairs = values.reshape(count // 2, 2, heads, width)
    return pairs[:, 0] + pairs[:, 1]


def across(column, count):
    width = column.shape[1]
    return jnp.concatenate([column] * (count // width), 1) if count > width else column


def with_ones(values):
    return jnp.concatenate([values, jnp.ones_like(values)], 1)


def kernel(size, q_ref, k_ref, v_ref, o_ref,
           far, tail, thru, sendp, eq, e0, e1, e2, before, fk,
           mask1, mask0, maskt, acc, top, total, tmp, otmp,
           recv, up_send, side_send, t_send, t_recv, r_send, r_recv):
    rows, heads, width = q_ref.shape
    own = rows // 8
    blocks = rows // BLOCK
    gain = math.log2(math.e) / math.sqrt(width)
    me = lax.axis_index("seq")
    col = lax.rem(me, 2)
    lev = me // 2
    levels = size // 2
    together = 2 - heads % 2
    groups = heads // together
    early = (groups + 1) // 2
    climbs = lev < levels - 1
    pair = me + 1 - 2 * col
    up = jnp.minimum(me + 2, size - 1)
    sources = (k_ref, v_ref)

    def remote(src, dst, send, got, target):
        return pltpu.make_async_remote_copy(
            src_ref=src, dst_ref=dst, send_sem=send, recv_sem=got,
            device_id={"seq": target}, device_id_type=pl.DeviceIdType.MESH)

    def up_copy(kv, b):
        return remote(far.at[kv, b], far.at[kv, b], up_send.at[kv, b], recv.at[kv, b], up)

    def side_copy(kv, b):
        return remote(far.at[kv, b], far.at[kv, b], side_send.at[kv, b], recv.at[kv, b], pair)

    def tail_source(kv, part):
        return sources[kv].at[pl.ds(rows - BLOCK, BLOCK)] if part == 0 else sendp.at[kv]

    def tail_copy(kv, part):
        return remote(tail_source(kv, part), tail.at[kv, part], t_send.at[kv, part], t_recv.at[kv, part], pair)

    def thru_copy(kv, part):
        return remote(tail_source(kv, part), thru.at[kv, part], t_send.at[kv, part], r_recv.at[kv, part], pair)

    def relay_copy(kv, part):
        return remote(thru.at[kv, part], tail.at[kv, part], r_send.at[kv, part], t_recv.at[kv, part], up)

    barrier = pltpu.get_barrier_semaphore()
    for step in (-2, 2):
        @pl.when((me + step >= 0) & (me + step < size))
        def _():
            pl.semaphore_signal(barrier, inc=1, device_id={"seq": me + step},
                                device_id_type=pl.DeviceIdType.MESH)
    pl.semaphore_signal(barrier, inc=1, device_id={"seq": pair}, device_id_type=pl.DeviceIdType.MESH)

    def split(kv, c):
        x = sources[kv][pl.ds(c * BLOCK, BLOCK)].astype(F32)
        two = halved(x)
        four = halved(two)
        eight = halved(four)
        far[kv, me, pl.ds(c * 8, 8)] = (eight * 0.125).astype(BF16)
        if c == blocks - 2:
            sendp[kv, pl.ds(0, 32)] = (two * 0.5).astype(BF16)
        if blocks - 4 <= c < blocks - 2:
            sendp[kv, pl.ds(32 + 16 * (c - blocks + 4), 16)] = (four * 0.25).astype(BF16)

    def spread(kv, c):
        x = sources[kv][pl.ds(c * BLOCK, BLOCK)].astype(F32)
        for h, part in enumerate(to_heads(x, tmp, heads)):
            e0[kv, h, pl.ds(c * BLOCK, BLOCK), :] = part
        if c < blocks - 2:
            two = halved(x)
            for h, part in enumerate(to_heads(two * 0.5, tmp, heads)):
                e1[kv, h, pl.ds(c * 32, 32), :] = part
            if c < blocks - 4:
                four = halved(two)
                for h, part in enumerate(to_heads(four * 0.25, tmp, heads)):
                    e2[kv, h, pl.ds(c * 16, 16), :] = part

    for kv in (1, 0):
        for c in range(blocks):
            split(kv, c)

    pl.semaphore_wait(barrier, 1 + jnp.where(lev > 0, 1, 0) + jnp.where(climbs, 1, 0))

    @pl.when(col == 0)
    def _():
        side_copy(1, me).start()
        side_copy(0, me).start()

        @pl.when(climbs)
        def _():
            up_copy(0, me).start()

        @pl.when(lev < levels - 2)
        def _():
            up_copy(1, me).start()

    @pl.when((col == 1) & climbs)
    def _():
        up_copy(0, me).start()
        up_copy(1, me).start()
        for kv in range(2):
            for part in range(2):
                thru_copy(kv, part).start()

    for kv in range(2):
        for c in range(blocks):
            spread(kv, c)
    for c in range(blocks):
        x = q_ref[pl.ds(c * BLOCK, BLOCK)].astype(F32)
        for h, part in enumerate(to_heads(x, tmp, heads)):
            eq[h, pl.ds(c * BLOCK, BLOCK), :] = part

    def grid(count):
        return (lax.broadcasted_iota(jnp.int32, (HALF, count), 0),
                lax.broadcasted_iota(jnp.int32, (HALF, count), 1))

    i, j = grid(NEAR)
    level = jnp.where(j < 192, 0.0, jnp.where(j < 256, 1.0, jnp.where(j < 320, 2.0, 3.0)))
    seen01 = jnp.where(j < 192, jnp.where((j <= i + BLOCK) & ((j >= BLOCK) | (i < BLOCK)), 1, 0),
                       jnp.where((j < 224) | (i >= BLOCK), 1, 0))
    for hf in range(2):
        seen = jnp.where(j < 256, seen01, jnp.where(j < 320, jnp.where((j < 288) | (hf == 1), 1, 0), col))
        mask1[hf] = jnp.where(seen > 0, level, NEG)
    i, j = grid(HALF)
    mask0[:, pl.ds(0, HALF)] = jnp.where(j <= i, 0.0, NEG)
    i, j = grid(2 * HALF)
    seen0 = jnp.where(j < 192, jnp.where((j <= i + BLOCK) & ((j >= BLOCK) | (i < BLOCK)), 1, 0),
                      jnp.where((j < 224) | (i >= BLOCK), 1, 0))
    mask0[:, pl.ds(HALF, 2 * HALF)] = jnp.where(seen0 > 0, jnp.where(j < 192, 0.0, 1.0), NEG)
    last = jnp.where(j < 192 + own // 2, col, 0)
    seent = jnp.where(j < 64, jnp.where(i < BLOCK, 1, 0),
                      jnp.where(j < 128, jnp.where((j < 96) | (i >= BLOCK), 1, 0),
                                jnp.where(j < 192, jnp.where(j < 160, 1, 0), last)))
    level = jnp.where(j < 64, 0.0, jnp.where(j < 128, 1.0, jnp.where(j < 192, 2.0, 3.0)))
    maskt[:, pl.ds(0, 2 * HALF)] = jnp.where(seent > 0, level, NEG)
    i, j = grid(HALF)
    maskt[:, pl.ds(2 * HALF, HALF)] = jnp.where(j < 64, 2.0, jnp.where((j < 64 + own // 2) & (col == 1), 3.0, NEG))

    def begin(h, at, kk, vv, mask):
        s = lax.dot_general(eq[h, pl.ds(at, HALF), :], kk, (((1,), (1,)), ((), ())),
                            preferred_element_type=F32)
        s = s * gain + mask
        m = jnp.broadcast_to(jnp.max(s, axis=1, keepdims=True), (HALF, width))
        w = jnp.exp2(s - across(m, s.shape[1])).astype(BF16)
        both = jnp.dot(w, with_ones(vv), preferred_element_type=F32)
        top[h, pl.ds(at, HALF), :] = m
        acc[h, pl.ds(at, HALF), :] = both[:, :width]
        total[h, pl.ds(at, HALF), :] = both[:, width:]

    def near(qd, first, count):
        def body(g, _):
            for part in range(2 * together):
                h, hf = g * together + part // 2, part % 2
                at = qd * QUAD + hf * HALF
                kk, vv = (jnp.concatenate([
                    e0[kv, h, pl.ds(at - BLOCK, 192), :],
                    e1[kv, h, pl.ds(at // 2 - BLOCK, BLOCK), :],
                    e2[kv, h, pl.ds((qd - 1) * BLOCK, BLOCK), :],
                    before[kv, h, pl.ds(3 * BLOCK, BLOCK)]], 0) for kv in range(2))
                begin(h, at, kk, vv, mask1[hf])
            return 0
        lax.fori_loop(first, first + count, body, 0)

    def nearest(first, count):
        def body(g, _):
            for n in range(together):
                h = g * together + n
                begin(h, 0, e0[0, h, pl.ds(0, HALF), :], e0[1, h, pl.ds(0, HALF), :], mask0[:, pl.ds(0, HALF)])
                kk, vv = (jnp.concatenate([
                    e0[kv, h, pl.ds(BLOCK, 192), :], e1[kv, h, pl.ds(0, BLOCK), :]], 0) for kv in range(2))
                begin(h, HALF, kk, vv, mask0[:, pl.ds(HALF, 2 * HALF)])
            return 0
        lax.fori_loop(first, first + count, body, 0)

    def merge(h, at, count, s, vv, lift):
        m = top[h, pl.ds(at, count), :]
        peak = jnp.max(s, axis=1, keepdims=True)
        if lift is not None:
            peak = peak * gain + lift
            s = s * gain
        fresh = jnp.maximum(m, peak)
        fade = jnp.exp2(m - fresh)
        w = jnp.exp2(s - across(fresh if lift is None else fresh - lift, s.shape[1])).astype(BF16)
        both = jnp.dot(w, with_ones(vv), preferred_element_type=F32)
        top[h, pl.ds(at, count), :] = fresh
        acc[h, pl.ds(at, count), :] = acc[h, pl.ds(at, count), :] * fade + both[:, :width]
        total[h, pl.ds(at, count), :] = total[h, pl.ds(at, count), :] * fade + both[:, width:]

    def scores(h, at, count, kk):
        return lax.dot_general(eq[h, pl.ds(at, count), :], kk, (((1,), (1,)), ((), ())),
                               preferred_element_type=F32)

    def extra():
        @pl.when(col == 1)
        def _():
            side_copy(0, me - 1).wait_recv()
            for kv in range(2):
                for h, part in enumerate(to_heads(far[kv, me - 1].astype(F32), tmp, heads)):
                    before[kv, h, pl.ds(3 * BLOCK, own)] = part

        @pl.when(col == 0)
        def _():
            for kv in range(2):
                for h in range(heads):
                    before[kv, h, pl.ds(3 * BLOCK, own)] = jnp.zeros((own, width), BF16)

    def previous():
        for kv in range(2):
            for part in range(2):
                tail_copy(kv, part).wait_recv()
            x = tail[kv, 0].astype(F32)
            two = halved(x)
            four = halved(two)
            y = tail[kv, 1].astype(F32)
            late = halved(y[:32])
            for h, part in enumerate(to_heads(x, tmp, heads)):
                before[kv, h, pl.ds(0, BLOCK), :] = part
            for h, part in enumerate(to_heads(two * 0.5, tmp, heads)):
                before[kv, h, pl.ds(96, 32), :] = part
            for h, part in enumerate(to_heads(four * 0.25, tmp, heads)):
                before[kv, h, pl.ds(176, 16), :] = part
            for h, part in enumerate(to_heads(late * 0.5, tmp, heads)):
                before[kv, h, pl.ds(160, 16), :] = part
            for h, part in enumerate(to_heads(y, tmp, heads)):
                before[kv, h, pl.ds(64, 32), :] = part[:32]
                before[kv, h, pl.ds(128, 32), :] = part[32:]

        def body(g, _):
            for n in range(together):
                h = g * together + n
                s = scores(h, 0, HALF, before[0, h]) * gain + maskt[:, pl.ds(0, 2 * HALF)]
                merge(h, 0, HALF, s, before[1, h], None)
                s = (scores(h, HALF, HALF, before[0, h, pl.ds(HALF, HALF), :]) * gain
                     + maskt[:, pl.ds(2 * HALF, HALF)])
                merge(h, HALF, HALF, s, before[1, h, pl.ds(HALF, HALF), :], None)
            return 0
        lax.fori_loop(0, groups, body, 0)

    def distant(r):
        odd = me - 2 * r + 1 - col
        even = me - 2 * r - col

        @pl.when(col == 1)
        def _():
            side_copy(0, even).wait_recv()

        @pl.when(col == 0)
        def _():
            side_copy(0, odd).wait_recv()
            side_copy(1, odd).wait_recv()

            @pl.when(jnp.logical_not(climbs))
            def _():
                side_copy(1, even).wait_recv()
        for kv in range(2):
            for n, b in enumerate((odd, even)):
                for h, part in enumerate(to_heads(far[kv, b].astype(F32), tmp, heads)):
                    fk[kv, h, pl.ds(n * own, own), :] = part
        place = lax.broadcasted_iota(jnp.int32, (1, 2 * own), 1)
        hide = jnp.where((col == 0) & (r == 1) & (place >= own // 2) & (place < own), NEG, 0.0)

        def body(g, _):
            for n in range(together * (rows // QUAD)):
                h, qd = g * together + n // (rows // QUAD), n % (rows // QUAD)
                at = qd * QUAD
                s = scores(h, at, QUAD, fk[0, h])
                if qd == 0:
                    s = s + hide
                merge(h, at, QUAD, s, fk[1, h], 3.0)
            return 0

        lax.fori_loop(0, heads // together, body, 0)

    def climb(kv, b):
        up_copy(kv, b).wait_recv()

        @pl.when(climbs)
        def _():
            up_copy(kv, b).start()

    def odd_turn(n):
        def at(turn, r):
            return (n == turn) & (r <= lev)

        @pl.when(n == 1)
        def _():
            climb(1, me - 1)

        for turn, r in ((1, 1), (4, 2), (6, 3)):
            @pl.when(at(turn, r))
            def _():
                climb(0, me - 2 * r)
                side_copy(0, me - 2 * r).start()

        for turn, r in ((2, 1), (5, 2), (6, 3)):
            @pl.when(at(turn, r))
            def _():
                climb(1, me - 2 * r)
                side_copy(1, me - 2 * r).start()

        for turn, r in ((3, 1), (5, 2), (7, 3)):
            @pl.when(at(turn, r))
            def _():
                climb(1, me - 2 * r - 1)
                if r == 1:
                    @pl.when(jnp.logical_not(climbs))
                    def _():
                        side_copy(1, me - 3).start()

        @pl.when((n >= 8) & (n - 4 <= lev))
        def _():
            b = me - 2 * (n - 4)
            for kv in range(2):
                climb(kv, b)
                side_copy(kv, b).start()
            climb(1, b - 1)

    def even_turn(n):
        def relay(kv, part):
            @pl.when(climbs)
            def _():
                thru_copy(kv, part).wait_recv()
                relay_copy(kv, part).start()

        def cross(r):
            @pl.when(r <= lev)
            def _():
                climb(0, me - 2 * r)
                side_copy(0, me - 2 * r).start()

        def rise(r):
            @pl.when((r <= lev) & climbs)
            def _():
                climb(1, me - 2 * r)

        @pl.when(n == 1)
        def _():
            cross(1)
            tail_copy(0, 0).start()
            tail_copy(0, 1).start()
            relay(0, 0)

        @pl.when(n == 2)
        def _():
            relay(0, 1)
            rise(1)

        @pl.when(n == 3)
        def _():
            cross(2)
            tail_copy(1, 0).start()
            tail_copy(1, 1).start()

        @pl.when(n == 4)
        def _():
            relay(1, 0)
            relay(1, 1)
            rise(2)

        @pl.when(n == 5)
        def _():
            cross(3)

        @pl.when(n == 7)
        def _():
            rise(3)

        @pl.when(n >= 8)
        def _():
            cross(n - 4)
            rise(n - 4)

    def turn(n, _):
        @pl.when(col == 1)
        def _():
            odd_turn(n)

        @pl.when(col == 0)
        def _():
            even_turn(n)

        first = jnp.where(lax.rem(n, 2) == 0, 0, early)
        count = jnp.where(lax.rem(n, 2) == 0, early, groups - early)

        @pl.when(n < 2)
        def _():
            nearest(first, count)

        @pl.when(n == 2)
        def _():
            extra()

        @pl.when((n == 2) | (n == 3))
        def _():
            for qd in range(1, rows // QUAD):
                near(qd, first, count)

        @pl.when((n == 6) & (me > 0))
        def _():
            previous()

        gone = jnp.where(n < 6, n - 3, n - 4)

        @pl.when((gone >= 1) & (gone <= lev) & (n != 6))
        def _():
            distant(gone)
        return 0

    lax.fori_loop(0, jnp.maximum(6, lev + 4) + 1, turn, 0)

    for c in range(rows // HALF):
        for h in range(heads):
            otmp[pl.ds(h, HALF, stride=heads), :] = (
                acc[h, pl.ds(c * HALF, HALF), :] / total[h, pl.ds(c * HALF, HALF), :])
        o_ref[pl.ds(c * HALF, HALF)] = otmp[...].reshape(HALF, heads, width).astype(BF16)

    @pl.when(col == 0)
    def _():
        side_copy(1, me).wait_send()
        side_copy(0, me).wait_send()
        for kv in range(2):
            for part in range(2):
                tail_copy(kv, part).wait_send()

        @pl.when(climbs)
        def _():
            up_copy(0, me).wait_send()
            for kv in range(2):
                for part in range(2):
                    relay_copy(kv, part).wait_send()

        @pl.when(lev < levels - 2)
        def _():
            up_copy(1, me).wait_send()

    @pl.when((col == 1) & climbs)
    def _():
        up_copy(0, me).wait_send()
        up_copy(1, me).wait_send()
        up_copy(1, me - 1).wait_send()
        for kv in range(2):
            for part in range(2):
                thru_copy(kv, part).wait_send()

    def sent(r, _):
        b = me - 2 * r
        side_copy(0, b).wait_send()

        @pl.when(climbs)
        def _():
            up_copy(0, b).wait_send()
            up_copy(1, b).wait_send()

        @pl.when(col == 1)
        def _():
            side_copy(1, b).wait_send()

            @pl.when(climbs)
            def _():
                up_copy(1, b - 1).wait_send()

            @pl.when((r == 1) & jnp.logical_not(climbs))
            def _():
                side_copy(1, b - 1).wait_send()
        return 0

    lax.fori_loop(1, lev + 1, sent, 0)


def shards(size, queries, keys, values):
    rows, heads, width = queries.shape
    own = rows // 8
    vmem = pl.BlockSpec(memory_space=pltpu.VMEM)
    return pl.pallas_call(
        functools.partial(kernel, size),
        out_shape=jax.ShapeDtypeStruct((rows, heads, width), BF16),
        in_specs=[vmem] * 3,
        out_specs=vmem,
        scratch_shapes=[
            pltpu.VMEM((2, size, own, heads, width), BF16),
            pltpu.VMEM((2, 2, BLOCK, heads, width), BF16),
            pltpu.VMEM((2, 2, BLOCK, heads, width), BF16),
            pltpu.VMEM((2, BLOCK, heads, width), BF16),
            pltpu.VMEM((heads, rows, width), BF16),
            pltpu.VMEM((2, heads, rows, width), BF16),
            pltpu.VMEM((2, heads, rows // 2 - BLOCK, width), BF16),
            pltpu.VMEM((2, heads, rows // 4 - BLOCK, width), BF16),
            pltpu.VMEM((2, heads, QUAD, width), BF16),
            pltpu.VMEM((2, heads, 2 * own, width), BF16),
            pltpu.VMEM((2, HALF, NEAR), F32),
            pltpu.VMEM((HALF, 3 * HALF), F32),
            pltpu.VMEM((HALF, 3 * HALF), F32),
            pltpu.VMEM((heads, rows, width), F32),
            pltpu.VMEM((heads, rows, width), F32),
            pltpu.VMEM((heads, rows, width), F32),
            pltpu.VMEM((80 * heads, width), F32),
            pltpu.VMEM((HALF * heads, width), F32),
            pltpu.SemaphoreType.DMA((2, size)),
            pltpu.SemaphoreType.DMA((2, size)),
            pltpu.SemaphoreType.DMA((2, size)),
            pltpu.SemaphoreType.DMA((2, 2)),
            pltpu.SemaphoreType.DMA((2, 2)),
            pltpu.SemaphoreType.DMA((2, 2)),
            pltpu.SemaphoreType.DMA((2, 2)),
        ],
        compiler_params=pltpu.CompilerParams(
            collective_id=0, has_side_effects=True, vmem_limit_bytes=60 * 2**20),
    )(queries, keys, values)


def solution(mesh):
    spec = P(("groups", "seq"), "heads", None)
    return jax.shard_map(
        functools.partial(shards, mesh.shape["seq"]),
        mesh=mesh, in_specs=(spec,) * 3, out_specs=spec, check_vma=False)
```

```python
import functools
import math

import jax
import jax.numpy as jnp
from jax import lax
from jax.experimental import pallas as pl
from jax.experimental.pallas import tpu as pltpu
from jax.sharding import PartitionSpec as P

BLOCK = 64
QUAD = 4 * BLOCK
HALF = 2 * BLOCK
NEAR = 6 * BLOCK
NEG = -1e30
F32 = jnp.float32
BF16 = jnp.bfloat16


def to_heads(values, scratch, heads):
    count, _, width = values.shape
    scratch[pl.ds(0, count * heads), :] = values.reshape(count * heads, width)
    return [scratch[pl.ds(h, count, stride=heads), :].astype(BF16) for h in range(heads)]


def halved(values):
    count, heads, width = values.shape
    pairs = values.reshape(count // 2, 2, heads, width)
    return pairs[:, 0] + pairs[:, 1]


def across(column, count):
    width = column.shape[1]
    return jnp.concatenate([column] * (count // width), 1) if count > width else column


def with_ones(values):
    return jnp.concatenate([values, jnp.ones_like(values)], 1)


def kernel(size, q_hbm, k_hbm, v_hbm, o_ref,
           q_ref, k_ref, v_ref, far, tail, thru, sendp, eq, e0, e1, e2, before, fk,
           mask1, mask0, maskt, acc, top, total, tmp, otmp,
           in_sem, recv, up_send, side_send, t_send, t_recv, r_send, r_recv):
    rows, heads, width = q_ref.shape
    own = rows // 8
    blocks = rows // BLOCK
    gain = math.log2(math.e) / math.sqrt(width)
    me = lax.axis_index("seq")
    col = lax.rem(me, 2)
    lev = me // 2
    levels = size // 2
    together = 2 - heads % 2
    groups = heads // together
    early = (groups + 1) // 2
    climbs = lev < levels - 1
    pair = me + 1 - 2 * col
    up = jnp.minimum(me + 2, size - 1)
    sources = (k_ref, v_ref)

    def remote(src, dst, send, got, target):
        return pltpu.make_async_remote_copy(
            src_ref=src, dst_ref=dst, send_sem=send, recv_sem=got,
            device_id={"seq": target}, device_id_type=pl.DeviceIdType.MESH)

    def up_copy(kv, b):
        return remote(far.at[kv, b], far.at[kv, b], up_send.at[kv, b], recv.at[kv, b], up)

    def side_copy(kv, b):
        return remote(far.at[kv, b], far.at[kv, b], side_send.at[kv, b], recv.at[kv, b], pair)

    def tail_source(kv, part):
        return sources[kv].at[pl.ds(rows - BLOCK, BLOCK)] if part == 0 else sendp.at[kv]

    def tail_copy(kv, part):
        return remote(tail_source(kv, part), tail.at[kv, part], t_send.at[kv, part], t_recv.at[kv, part], pair)

    def thru_copy(kv, part):
        return remote(tail_source(kv, part), thru.at[kv, part], t_send.at[kv, part], r_recv.at[kv, part], pair)

    def relay_copy(kv, part):
        return remote(thru.at[kv, part], tail.at[kv, part], r_send.at[kv, part], t_recv.at[kv, part], up)

    barrier = pltpu.get_barrier_semaphore()
    for step in (-2, 2):
        @pl.when((me + step >= 0) & (me + step < size))
        def _():
            pl.semaphore_signal(barrier, inc=1, device_id={"seq": me + step},
                                device_id_type=pl.DeviceIdType.MESH)
    pl.semaphore_signal(barrier, inc=1, device_id={"seq": pair}, device_id_type=pl.DeviceIdType.MESH)

    loads = [pltpu.make_async_copy(src, dst, in_sem.at[n]) for n, (src, dst) in enumerate(
        ((v_hbm, v_ref), (k_hbm, k_ref), (q_hbm, q_ref)))]
    for load in loads:
        load.start()

    def split(kv, c):
        x = sources[kv][pl.ds(c * BLOCK, BLOCK)].astype(F32)
        two = halved(x)
        four = halved(two)
        eight = halved(four)
        far[kv, me, pl.ds(c * 8, 8)] = (eight * 0.125).astype(BF16)
        if c == blocks - 2:
            sendp[kv, pl.ds(0, 32)] = (two * 0.5).astype(BF16)
        if blocks - 4 <= c < blocks - 2:
            sendp[kv, pl.ds(32 + 16 * (c - blocks + 4), 16)] = (four * 0.25).astype(BF16)

    def spread(kv, c):
        x = sources[kv][pl.ds(c * BLOCK, BLOCK)].astype(F32)
        for h, part in enumerate(to_heads(x, tmp, heads)):
            e0[kv, h, pl.ds(c * BLOCK, BLOCK), :] = part
        if c < blocks - 2:
            two = halved(x)
            for h, part in enumerate(to_heads(two * 0.5, tmp, heads)):
                e1[kv, h, pl.ds(c * 32, 32), :] = part
            if c < blocks - 4:
                four = halved(two)
                for h, part in enumerate(to_heads(four * 0.25, tmp, heads)):
                    e2[kv, h, pl.ds(c * 16, 16), :] = part

    for kv in (1, 0):
        loads[1 - kv].wait()
        for c in range(blocks):
            split(kv, c)

    pl.semaphore_wait(barrier, 1 + jnp.where(lev > 0, 1, 0) + jnp.where(climbs, 1, 0))

    @pl.when(col == 0)
    def _():
        side_copy(1, me).start()
        side_copy(0, me).start()

        @pl.when(climbs)
        def _():
            up_copy(0, me).start()

        @pl.when(lev < levels - 2)
        def _():
            up_copy(1, me).start()

    @pl.when((col == 1) & climbs)
    def _():
        up_copy(0, me).start()
        up_copy(1, me).start()
        for kv in range(2):
            for part in range(2):
                thru_copy(kv, part).start()

    for kv in range(2):
        for c in range(blocks):
            spread(kv, c)
    loads[2].wait()
    for c in range(blocks):
        x = q_ref[pl.ds(c * BLOCK, BLOCK)].astype(F32)
        for h, part in enumerate(to_heads(x, tmp, heads)):
            eq[h, pl.ds(c * BLOCK, BLOCK), :] = part

    def grid(count):
        return (lax.broadcasted_iota(jnp.int32, (HALF, count), 0),
                lax.broadcasted_iota(jnp.int32, (HALF, count), 1))

    i, j = grid(NEAR)
    level = jnp.where(j < 192, 0.0, jnp.where(j < 256, 1.0, jnp.where(j < 320, 2.0, 3.0)))
    seen01 = jnp.where(j < 192, jnp.where((j <= i + BLOCK) & ((j >= BLOCK) | (i < BLOCK)), 1, 0),
                       jnp.where((j < 224) | (i >= BLOCK), 1, 0))
    for hf in range(2):
        seen = jnp.where(j < 256, seen01, jnp.where(j < 320, jnp.where((j < 288) | (hf == 1), 1, 0), col))
        mask1[hf] = jnp.where(seen > 0, level, NEG)
    i, j = grid(HALF)
    mask0[:, pl.ds(0, HALF)] = jnp.where(j <= i, 0.0, NEG)
    i, j = grid(2 * HALF)
    seen0 = jnp.where(j < 192, jnp.where((j <= i + BLOCK) & ((j >= BLOCK) | (i < BLOCK)), 1, 0),
                      jnp.where((j < 224) | (i >= BLOCK), 1, 0))
    mask0[:, pl.ds(HALF, 2 * HALF)] = jnp.where(seen0 > 0, jnp.where(j < 192, 0.0, 1.0), NEG)
    last = jnp.where(j < 192 + own // 2, col, 0)
    seent = jnp.where(j < 64, jnp.where(i < BLOCK, 1, 0),
                      jnp.where(j < 128, jnp.where((j < 96) | (i >= BLOCK), 1, 0),
                                jnp.where(j < 192, jnp.where(j < 160, 1, 0), last)))
    level = jnp.where(j < 64, 0.0, jnp.where(j < 128, 1.0, jnp.where(j < 192, 2.0, 3.0)))
    maskt[:, pl.ds(0, 2 * HALF)] = jnp.where(seent > 0, level, NEG)
    i, j = grid(HALF)
    maskt[:, pl.ds(2 * HALF, HALF)] = jnp.where(j < 64, 2.0, jnp.where((j < 64 + own // 2) & (col == 1), 3.0, NEG))

    def begin(h, at, kk, vv, mask):
        s = lax.dot_general(eq[h, pl.ds(at, HALF), :], kk, (((1,), (1,)), ((), ())),
                            preferred_element_type=F32)
        s = s * gain + mask
        m = jnp.broadcast_to(jnp.max(s, axis=1, keepdims=True), (HALF, width))
        w = jnp.exp2(s - across(m, s.shape[1])).astype(BF16)
        both = jnp.dot(w, with_ones(vv), preferred_element_type=F32)
        top[h, pl.ds(at, HALF), :] = m
        acc[h, pl.ds(at, HALF), :] = both[:, :width]
        total[h, pl.ds(at, HALF), :] = both[:, width:]

    def near(qd, first, count):
        def body(g, _):
            for part in range(2 * together):
                h, hf = g * together + part // 2, part % 2
                at = qd * QUAD + hf * HALF
                kk, vv = (jnp.concatenate([
                    e0[kv, h, pl.ds(at - BLOCK, 192), :],
                    e1[kv, h, pl.ds(at // 2 - BLOCK, BLOCK), :],
                    e2[kv, h, pl.ds((qd - 1) * BLOCK, BLOCK), :],
                    before[kv, h, pl.ds(3 * BLOCK, BLOCK)]], 0) for kv in range(2))
                begin(h, at, kk, vv, mask1[hf])
            return 0
        lax.fori_loop(first, first + count, body, 0)

    def nearest(first, count):
        def body(g, _):
            for n in range(together):
                h = g * together + n
                begin(h, 0, e0[0, h, pl.ds(0, HALF), :], e0[1, h, pl.ds(0, HALF), :], mask0[:, pl.ds(0, HALF)])
                kk, vv = (jnp.concatenate([
                    e0[kv, h, pl.ds(BLOCK, 192), :], e1[kv, h, pl.ds(0, BLOCK), :]], 0) for kv in range(2))
                begin(h, HALF, kk, vv, mask0[:, pl.ds(HALF, 2 * HALF)])
            return 0
        lax.fori_loop(first, first + count, body, 0)

    def merge(h, at, count, s, vv, lift):
        m = top[h, pl.ds(at, count), :]
        peak = jnp.max(s, axis=1, keepdims=True)
        if lift is not None:
            peak = peak * gain + lift
            s = s * gain
        fresh = jnp.maximum(m, peak)
        fade = jnp.exp2(m - fresh)
        w = jnp.exp2(s - across(fresh if lift is None else fresh - lift, s.shape[1])).astype(BF16)
        both = jnp.dot(w, with_ones(vv), preferred_element_type=F32)
        top[h, pl.ds(at, count), :] = fresh
        acc[h, pl.ds(at, count), :] = acc[h, pl.ds(at, count), :] * fade + both[:, :width]
        total[h, pl.ds(at, count), :] = total[h, pl.ds(at, count), :] * fade + both[:, width:]

    def scores(h, at, count, kk):
        return lax.dot_general(eq[h, pl.ds(at, count), :], kk, (((1,), (1,)), ((), ())),
                               preferred_element_type=F32)

    def extra():
        @pl.when(col == 1)
        def _():
            side_copy(0, me - 1).wait_recv()
            for kv in range(2):
                for h, part in enumerate(to_heads(far[kv, me - 1].astype(F32), tmp, heads)):
                    before[kv, h, pl.ds(3 * BLOCK, own)] = part

        @pl.when(col == 0)
        def _():
            for kv in range(2):
                for h in range(heads):
                    before[kv, h, pl.ds(3 * BLOCK, own)] = jnp.zeros((own, width), BF16)

    def previous():
        for kv in range(2):
            for part in range(2):
                tail_copy(kv, part).wait_recv()
            x = tail[kv, 0].astype(F32)
            two = halved(x)
            four = halved(two)
            y = tail[kv, 1].astype(F32)
            late = halved(y[:32])
            for h, part in enumerate(to_heads(x, tmp, heads)):
                before[kv, h, pl.ds(0, BLOCK), :] = part
            for h, part in enumerate(to_heads(two * 0.5, tmp, heads)):
                before[kv, h, pl.ds(96, 32), :] = part
            for h, part in enumerate(to_heads(four * 0.25, tmp, heads)):
                before[kv, h, pl.ds(176, 16), :] = part
            for h, part in enumerate(to_heads(late * 0.5, tmp, heads)):
                before[kv, h, pl.ds(160, 16), :] = part
            for h, part in enumerate(to_heads(y, tmp, heads)):
                before[kv, h, pl.ds(64, 32), :] = part[:32]
                before[kv, h, pl.ds(128, 32), :] = part[32:]

        def body(g, _):
            for n in range(together):
                h = g * together + n
                s = scores(h, 0, HALF, before[0, h]) * gain + maskt[:, pl.ds(0, 2 * HALF)]
                merge(h, 0, HALF, s, before[1, h], None)
                s = (scores(h, HALF, HALF, before[0, h, pl.ds(HALF, HALF), :]) * gain
                     + maskt[:, pl.ds(2 * HALF, HALF)])
                merge(h, HALF, HALF, s, before[1, h, pl.ds(HALF, HALF), :], None)
            return 0
        lax.fori_loop(0, groups, body, 0)

    def distant(r):
        odd = me - 2 * r + 1 - col
        even = me - 2 * r - col

        @pl.when(col == 1)
        def _():
            side_copy(0, even).wait_recv()

        @pl.when(col == 0)
        def _():
            side_copy(0, odd).wait_recv()
            side_copy(1, odd).wait_recv()

            @pl.when(jnp.logical_not(climbs))
            def _():
                side_copy(1, even).wait_recv()
        for kv in range(2):
            for n, b in enumerate((odd, even)):
                for h, part in enumerate(to_heads(far[kv, b].astype(F32), tmp, heads)):
                    fk[kv, h, pl.ds(n * own, own), :] = part
        place = lax.broadcasted_iota(jnp.int32, (1, 2 * own), 1)
        hide = jnp.where((col == 0) & (r == 1) & (place >= own // 2) & (place < own), NEG, 0.0)

        def body(g, _):
            for n in range(together * (rows // QUAD)):
                h, qd = g * together + n // (rows // QUAD), n % (rows // QUAD)
                at = qd * QUAD
                s = scores(h, at, QUAD, fk[0, h])
                if qd == 0:
                    s = s + hide
                merge(h, at, QUAD, s, fk[1, h], 3.0)
            return 0

        lax.fori_loop(0, heads // together, body, 0)

    def climb(kv, b):
        up_copy(kv, b).wait_recv()

        @pl.when(climbs)
        def _():
            up_copy(kv, b).start()

    def odd_turn(n):
        def at(turn, r):
            return (n == turn) & (r <= lev)

        @pl.when(n == 1)
        def _():
            climb(1, me - 1)

        for turn, r in ((1, 1), (4, 2), (6, 3)):
            @pl.when(at(turn, r))
            def _():
                climb(0, me - 2 * r)
                side_copy(0, me - 2 * r).start()

        for turn, r in ((2, 1), (5, 2), (6, 3)):
            @pl.when(at(turn, r))
            def _():
                climb(1, me - 2 * r)
                side_copy(1, me - 2 * r).start()

        for turn, r in ((3, 1), (5, 2), (7, 3)):
            @pl.when(at(turn, r))
            def _():
                climb(1, me - 2 * r - 1)
                if r == 1:
                    @pl.when(jnp.logical_not(climbs))
                    def _():
                        side_copy(1, me - 3).start()

        @pl.when((n >= 8) & (n - 4 <= lev))
        def _():
            b = me - 2 * (n - 4)
            for kv in range(2):
                climb(kv, b)
                side_copy(kv, b).start()
            climb(1, b - 1)

    def even_turn(n):
        def relay(kv, part):
            @pl.when(climbs)
            def _():
                thru_copy(kv, part).wait_recv()
                relay_copy(kv, part).start()

        def cross(r):
            @pl.when(r <= lev)
            def _():
                climb(0, me - 2 * r)
                side_copy(0, me - 2 * r).start()

        def rise(r):
            @pl.when((r <= lev) & climbs)
            def _():
                climb(1, me - 2 * r)

        @pl.when(n == 1)
        def _():
            cross(1)
            tail_copy(0, 0).start()
            tail_copy(0, 1).start()
            relay(0, 0)

        @pl.when(n == 2)
        def _():
            relay(0, 1)
            rise(1)

        @pl.when(n == 3)
        def _():
            cross(2)
            tail_copy(1, 0).start()
            tail_copy(1, 1).start()

        @pl.when(n == 4)
        def _():
            relay(1, 0)
            relay(1, 1)
            rise(2)

        @pl.when(n == 5)
        def _():
            cross(3)

        @pl.when(n == 7)
        def _():
            rise(3)

        @pl.when(n >= 8)
        def _():
            cross(n - 4)
            rise(n - 4)

    def turn(n, _):
        @pl.when(col == 1)
        def _():
            odd_turn(n)

        @pl.when(col == 0)
        def _():
            even_turn(n)

        first = jnp.where(lax.rem(n, 2) == 0, 0, early)
        count = jnp.where(lax.rem(n, 2) == 0, early, groups - early)

        @pl.when(n < 2)
        def _():
            nearest(first, count)

        @pl.when(n == 2)
        def _():
            extra()

        @pl.when((n == 2) | (n == 3))
        def _():
            for qd in range(1, rows // QUAD):
                near(qd, first, count)

        @pl.when((n == 6) & (me > 0))
        def _():
            previous()

        gone = jnp.where(n < 6, n - 3, n - 4)

        @pl.when((gone >= 1) & (gone <= lev) & (n != 6))
        def _():
            distant(gone)
        return 0

    lax.fori_loop(0, jnp.maximum(6, lev + 4) + 1, turn, 0)

    for c in range(rows // HALF):
        for h in range(heads):
            otmp[pl.ds(h, HALF, stride=heads), :] = (
                acc[h, pl.ds(c * HALF, HALF), :] / total[h, pl.ds(c * HALF, HALF), :])
        o_ref[pl.ds(c * HALF, HALF)] = otmp[...].reshape(HALF, heads, width).astype(BF16)

    @pl.when(col == 0)
    def _():
        side_copy(1, me).wait_send()
        side_copy(0, me).wait_send()
        for kv in range(2):
            for part in range(2):
                tail_copy(kv, part).wait_send()

        @pl.when(climbs)
        def _():
            up_copy(0, me).wait_send()
            for kv in range(2):
                for part in range(2):
                    relay_copy(kv, part).wait_send()

        @pl.when(lev < levels - 2)
        def _():
            up_copy(1, me).wait_send()

    @pl.when((col == 1) & climbs)
    def _():
        up_copy(0, me).wait_send()
        up_copy(1, me).wait_send()
        up_copy(1, me - 1).wait_send()
        for kv in range(2):
            for part in range(2):
                thru_copy(kv, part).wait_send()

    def sent(r, _):
        b = me - 2 * r
        side_copy(0, b).wait_send()

        @pl.when(climbs)
        def _():
            up_copy(0, b).wait_send()
            up_copy(1, b).wait_send()

        @pl.when(col == 1)
        def _():
            side_copy(1, b).wait_send()

            @pl.when(climbs)
            def _():
                up_copy(1, b - 1).wait_send()

            @pl.when((r == 1) & jnp.logical_not(climbs))
            def _():
                side_copy(1, b - 1).wait_send()
        return 0

    lax.fori_loop(1, lev + 1, sent, 0)


def shards(size, queries, keys, values):
    rows, heads, width = queries.shape
    own = rows // 8
    vmem = pl.BlockSpec(memory_space=pltpu.VMEM)
    return pl.pallas_call(
        functools.partial(kernel, size),
        out_shape=pltpu.VMEM((rows, heads, width), BF16),
        in_specs=[pl.BlockSpec(memory_space=pl.ANY)] * 3,
        out_specs=vmem,
        scratch_shapes=[
            pltpu.VMEM((rows, heads, width), BF16),
            pltpu.VMEM((rows, heads, width), BF16),
            pltpu.VMEM((rows, heads, width), BF16),
            pltpu.VMEM((2, size, own, heads, width), BF16),
            pltpu.VMEM((2, 2, BLOCK, heads, width), BF16),
            pltpu.VMEM((2, 2, BLOCK, heads, width), BF16),
            pltpu.VMEM((2, BLOCK, heads, width), BF16),
            pltpu.VMEM((heads, rows, width), BF16),
            pltpu.VMEM((2, heads, rows, width), BF16),
            pltpu.VMEM((2, heads, rows // 2 - BLOCK, width), BF16),
            pltpu.VMEM((2, heads, rows // 4 - BLOCK, width), BF16),
            pltpu.VMEM((2, heads, QUAD, width), BF16),
            pltpu.VMEM((2, heads, 2 * own, width), BF16),
            pltpu.VMEM((2, HALF, NEAR), F32),
            pltpu.VMEM((HALF, 3 * HALF), F32),
            pltpu.VMEM((HALF, 3 * HALF), F32),
            pltpu.VMEM((heads, rows, width), F32),
            pltpu.VMEM((heads, rows, width), F32),
            pltpu.VMEM((heads, rows, width), F32),
            pltpu.VMEM((80 * heads, width), F32),
            pltpu.VMEM((HALF * heads, width), F32),
            pltpu.SemaphoreType.DMA((3,)),
            pltpu.SemaphoreType.DMA((2, size)),
            pltpu.SemaphoreType.DMA((2, size)),
            pltpu.SemaphoreType.DMA((2, size)),
            pltpu.SemaphoreType.DMA((2, 2)),
            pltpu.SemaphoreType.DMA((2, 2)),
            pltpu.SemaphoreType.DMA((2, 2)),
            pltpu.SemaphoreType.DMA((2, 2)),
        ],
        compiler_params=pltpu.CompilerParams(
            collective_id=0, has_side_effects=True, vmem_limit_bytes=60 * 2**20),
    )(queries, keys, values)


def solution(mesh):
    spec = P(("groups", "seq"), "heads", None)
    return jax.shard_map(
        functools.partial(shards, mesh.shape["seq"]),
        mesh=mesh, in_specs=(spec,) * 3, out_specs=spec, check_vma=False)
```

```python
import functools
import math

import jax
import jax.numpy as jnp
from jax import lax
from jax.experimental import pallas as pl
from jax.experimental.pallas import tpu as pltpu
from jax.sharding import PartitionSpec as P

BLOCK = 64
QUAD = 4 * BLOCK
HALF = 2 * BLOCK
NEAR = 6 * BLOCK
NEG = -1e30
F32 = jnp.float32
BF16 = jnp.bfloat16


def to_heads(values, scratch, heads):
    count, _, width = values.shape
    scratch[pl.ds(0, count * heads), :] = values.reshape(count * heads, width)
    return [scratch[pl.ds(h, count, stride=heads), :].astype(BF16) for h in range(heads)]


def halved(values):
    count, heads, width = values.shape
    pairs = values.reshape(count // 2, 2, heads, width)
    return pairs[:, 0] + pairs[:, 1]


def across(column, count):
    width = column.shape[1]
    return jnp.concatenate([column] * (count // width), 1) if count > width else column


def with_ones(values):
    return jnp.concatenate([values, jnp.ones_like(values)], 1)


def kernel(size, q_hbm, k_hbm, v_hbm, o_ref,
           q_ref, k_ref, v_ref, far, tail, thru, sendp, eq, e0, e1, e2, before, fk,
           mask1, mask0, maskt, acc, top, total, tmp, otmp,
           in_sem, recv, up_send, side_send, t_send, t_recv, r_send, r_recv):
    rows, heads, width = q_ref.shape
    own = rows // 8
    blocks = rows // BLOCK
    gain = math.log2(math.e) / math.sqrt(width)
    me = lax.axis_index("seq")
    col = lax.rem(me, 2)
    lev = me // 2
    levels = size // 2
    together = 2 - heads % 2
    groups = heads // together
    early = (groups + 1) // 2
    share = heads // together
    climbs = lev < levels - 1
    pair = me + 1 - 2 * col
    up = jnp.minimum(me + 2, size - 1)
    sources = (k_ref, v_ref)

    def remote(src, dst, send, got, target):
        return pltpu.make_async_remote_copy(
            src_ref=src, dst_ref=dst, send_sem=send, recv_sem=got,
            device_id={"seq": target}, device_id_type=pl.DeviceIdType.MESH)

    def up_copy(kv, b, hh):
        place = far.at[kv, hh, b]
        return remote(place, place, up_send.at[kv, hh, b], recv.at[kv, hh, b], up)

    def side_copy(kv, b, hh):
        place = far.at[kv, hh, b]
        return remote(place, place, side_send.at[kv, hh, b], recv.at[kv, hh, b], pair)

    def every(copy, kv, b, action):
        for hh in range(together):
            getattr(copy(kv, b, hh), action)()

    def tail_source(kv, part):
        return sources[kv].at[pl.ds(rows - BLOCK, BLOCK)] if part == 0 else sendp.at[kv]

    def tail_copy(kv, part):
        return remote(tail_source(kv, part), tail.at[kv, part], t_send.at[kv, part], t_recv.at[kv, part], pair)

    def thru_copy(kv, part):
        return remote(tail_source(kv, part), thru.at[kv, part], t_send.at[kv, part], r_recv.at[kv, part], pair)

    def relay_copy(kv, part):
        return remote(thru.at[kv, part], tail.at[kv, part], r_send.at[kv, part], t_recv.at[kv, part], up)

    barrier = pltpu.get_barrier_semaphore()
    for step in (-2, 2):
        @pl.when((me + step >= 0) & (me + step < size))
        def _():
            pl.semaphore_signal(barrier, inc=1, device_id={"seq": me + step},
                                device_id_type=pl.DeviceIdType.MESH)
    pl.semaphore_signal(barrier, inc=1, device_id={"seq": pair}, device_id_type=pl.DeviceIdType.MESH)

    loads = [pltpu.make_async_copy(src, dst, in_sem.at[n]) for n, (src, dst) in enumerate(
        ((v_hbm, v_ref), (k_hbm, k_ref), (q_hbm, q_ref)))]
    for load in loads:
        load.start()

    def split(kv, c):
        x = sources[kv][pl.ds(c * BLOCK, BLOCK)].astype(F32)
        two = halved(x)
        four = halved(two)
        eight = halved(four)
        eight = (eight * 0.125).astype(BF16)
        for hh in range(together):
            far[kv, hh, me, pl.ds(c * 8, 8)] = eight[:, hh * share:(hh + 1) * share]
        if c == blocks - 2:
            sendp[kv, pl.ds(0, 32)] = (two * 0.5).astype(BF16)
        if blocks - 4 <= c < blocks - 2:
            sendp[kv, pl.ds(32 + 16 * (c - blocks + 4), 16)] = (four * 0.25).astype(BF16)

    def spread(kv, c):
        x = sources[kv][pl.ds(c * BLOCK, BLOCK)].astype(F32)
        for h, part in enumerate(to_heads(x, tmp, heads)):
            e0[kv, h, pl.ds(c * BLOCK, BLOCK), :] = part
        if c < blocks - 2:
            two = halved(x)
            for h, part in enumerate(to_heads(two * 0.5, tmp, heads)):
                e1[kv, h, pl.ds(c * 32, 32), :] = part
            if c < blocks - 4:
                four = halved(two)
                for h, part in enumerate(to_heads(four * 0.25, tmp, heads)):
                    e2[kv, h, pl.ds(c * 16, 16), :] = part

    for kv in (1, 0):
        loads[1 - kv].wait()
        for c in range(blocks):
            split(kv, c)

    pl.semaphore_wait(barrier, 1 + jnp.where(lev > 0, 1, 0) + jnp.where(climbs, 1, 0))

    @pl.when(col == 0)
    def _():
        every(side_copy, 1, me, "start")
        every(side_copy, 0, me, "start")

        @pl.when(climbs)
        def _():
            every(up_copy, 0, me, "start")

        @pl.when(lev < levels - 2)
        def _():
            every(up_copy, 1, me, "start")

    @pl.when((col == 1) & climbs)
    def _():
        every(up_copy, 0, me, "start")
        every(up_copy, 1, me, "start")
        for kv in range(2):
            for part in range(2):
                thru_copy(kv, part).start()

    for kv in range(2):
        for c in range(blocks):
            spread(kv, c)
    loads[2].wait()
    for c in range(blocks):
        x = q_ref[pl.ds(c * BLOCK, BLOCK)].astype(F32)
        for h, part in enumerate(to_heads(x, tmp, heads)):
            eq[h, pl.ds(c * BLOCK, BLOCK), :] = part

    def grid(count):
        return (lax.broadcasted_iota(jnp.int32, (HALF, count), 0),
                lax.broadcasted_iota(jnp.int32, (HALF, count), 1))

    i, j = grid(NEAR)
    level = jnp.where(j < 192, 0.0, jnp.where(j < 256, 1.0, jnp.where(j < 320, 2.0, 3.0)))
    seen01 = jnp.where(j < 192, jnp.where((j <= i + BLOCK) & ((j >= BLOCK) | (i < BLOCK)), 1, 0),
                       jnp.where((j < 224) | (i >= BLOCK), 1, 0))
    for hf in range(2):
        seen = jnp.where(j < 256, seen01, jnp.where(j < 320, jnp.where((j < 288) | (hf == 1), 1, 0), col))
        mask1[hf] = jnp.where(seen > 0, level, NEG)
    i, j = grid(HALF)
    mask0[:, pl.ds(0, HALF)] = jnp.where(j <= i, 0.0, NEG)
    i, j = grid(2 * HALF)
    seen0 = jnp.where(j < 192, jnp.where((j <= i + BLOCK) & ((j >= BLOCK) | (i < BLOCK)), 1, 0),
                      jnp.where((j < 224) | (i >= BLOCK), 1, 0))
    mask0[:, pl.ds(HALF, 2 * HALF)] = jnp.where(seen0 > 0, jnp.where(j < 192, 0.0, 1.0), NEG)
    last = jnp.where(j < 192 + own // 2, col, 0)
    seent = jnp.where(j < 64, jnp.where(i < BLOCK, 1, 0),
                      jnp.where(j < 128, jnp.where((j < 96) | (i >= BLOCK), 1, 0),
                                jnp.where(j < 192, jnp.where(j < 160, 1, 0), last)))
    level = jnp.where(j < 64, 0.0, jnp.where(j < 128, 1.0, jnp.where(j < 192, 2.0, 3.0)))
    maskt[:, pl.ds(0, 2 * HALF)] = jnp.where(seent > 0, level, NEG)
    i, j = grid(HALF)
    maskt[:, pl.ds(2 * HALF, HALF)] = jnp.where(j < 64, 2.0, jnp.where((j < 64 + own // 2) & (col == 1), 3.0, NEG))

    def begin(h, at, kk, vv, mask):
        s = lax.dot_general(eq[h, pl.ds(at, HALF), :], kk, (((1,), (1,)), ((), ())),
                            preferred_element_type=F32)
        s = s * gain + mask
        m = jnp.broadcast_to(jnp.max(s, axis=1, keepdims=True), (HALF, width))
        w = jnp.exp2(s - across(m, s.shape[1])).astype(BF16)
        both = jnp.dot(w, with_ones(vv), preferred_element_type=F32)
        top[h, pl.ds(at, HALF), :] = m
        acc[h, pl.ds(at, HALF), :] = both[:, :width]
        total[h, pl.ds(at, HALF), :] = both[:, width:]

    def near(qd, first, count):
        def body(g, _):
            for part in range(2 * together):
                h, hf = g * together + part // 2, part % 2
                at = qd * QUAD + hf * HALF
                kk, vv = (jnp.concatenate([
                    e0[kv, h, pl.ds(at - BLOCK, 192), :],
                    e1[kv, h, pl.ds(at // 2 - BLOCK, BLOCK), :],
                    e2[kv, h, pl.ds((qd - 1) * BLOCK, BLOCK), :],
                    before[kv, h, pl.ds(3 * BLOCK, BLOCK)]], 0) for kv in range(2))
                begin(h, at, kk, vv, mask1[hf])
            return 0
        lax.fori_loop(first, first + count, body, 0)

    def nearest(first, count):
        def body(g, _):
            for n in range(together):
                h = g * together + n
                begin(h, 0, e0[0, h, pl.ds(0, HALF), :], e0[1, h, pl.ds(0, HALF), :], mask0[:, pl.ds(0, HALF)])
                kk, vv = (jnp.concatenate([
                    e0[kv, h, pl.ds(BLOCK, 192), :], e1[kv, h, pl.ds(0, BLOCK), :]], 0) for kv in range(2))
                begin(h, HALF, kk, vv, mask0[:, pl.ds(HALF, 2 * HALF)])
            return 0
        lax.fori_loop(first, first + count, body, 0)

    def merge(h, at, count, s, vv, lift):
        m = top[h, pl.ds(at, count), :]
        peak = jnp.max(s, axis=1, keepdims=True)
        if lift is not None:
            peak = peak * gain + lift
            s = s * gain
        fresh = jnp.maximum(m, peak)
        fade = jnp.exp2(m - fresh)
        w = jnp.exp2(s - across(fresh if lift is None else fresh - lift, s.shape[1])).astype(BF16)
        both = jnp.dot(w, with_ones(vv), preferred_element_type=F32)
        top[h, pl.ds(at, count), :] = fresh
        acc[h, pl.ds(at, count), :] = acc[h, pl.ds(at, count), :] * fade + both[:, :width]
        total[h, pl.ds(at, count), :] = total[h, pl.ds(at, count), :] * fade + both[:, width:]

    def scores(h, at, count, kk):
        return lax.dot_general(eq[h, pl.ds(at, count), :], kk, (((1,), (1,)), ((), ())),
                               preferred_element_type=F32)

    def extra():
        @pl.when(col == 1)
        def _():
            every(side_copy, 0, me - 1, "wait_recv")
            for kv in range(2):
                for hh in range(together):
                    for h, part in enumerate(to_heads(far[kv, hh, me - 1].astype(F32), tmp, share)):
                        before[kv, hh * share + h, pl.ds(3 * BLOCK, own)] = part

        @pl.when(col == 0)
        def _():
            for kv in range(2):
                for h in range(heads):
                    before[kv, h, pl.ds(3 * BLOCK, own)] = jnp.zeros((own, width), BF16)

    def previous():
        for kv in range(2):
            for part in range(2):
                tail_copy(kv, part).wait_recv()
            x = tail[kv, 0].astype(F32)
            two = halved(x)
            four = halved(two)
            y = tail[kv, 1].astype(F32)
            late = halved(y[:32])
            for h, part in enumerate(to_heads(x, tmp, heads)):
                before[kv, h, pl.ds(0, BLOCK), :] = part
            for h, part in enumerate(to_heads(two * 0.5, tmp, heads)):
                before[kv, h, pl.ds(96, 32), :] = part
            for h, part in enumerate(to_heads(four * 0.25, tmp, heads)):
                before[kv, h, pl.ds(176, 16), :] = part
            for h, part in enumerate(to_heads(late * 0.5, tmp, heads)):
                before[kv, h, pl.ds(160, 16), :] = part
            for h, part in enumerate(to_heads(y, tmp, heads)):
                before[kv, h, pl.ds(64, 32), :] = part[:32]
                before[kv, h, pl.ds(128, 32), :] = part[32:]

        def body(g, _):
            for n in range(together):
                h = g * together + n
                s = scores(h, 0, HALF, before[0, h]) * gain + maskt[:, pl.ds(0, 2 * HALF)]
                merge(h, 0, HALF, s, before[1, h], None)
                s = (scores(h, HALF, HALF, before[0, h, pl.ds(HALF, HALF), :]) * gain
                     + maskt[:, pl.ds(2 * HALF, HALF)])
                merge(h, HALF, HALF, s, before[1, h, pl.ds(HALF, HALF), :], None)
            return 0
        lax.fori_loop(0, groups, body, 0)

    def distant(lower):
        upper = jnp.minimum(lower + 1, lev)
        place = lax.broadcasted_iota(jnp.int32, (1, 4 * own), 1)
        gone = (place >= 2 * own) & (upper == lower)
        inner = (col == 0) & (lower == 1) & (place >= own // 2) & (place < own)
        hides = [jnp.where(gone | inner, NEG, 0.0), jnp.where(gone, NEG, 0.0)]

        def fetch(r, hh, spot):
            odd = me - 2 * r + 1 - col
            even = me - 2 * r - col

            @pl.when((spot == 0) | (upper > lower))
            def _():
                @pl.when(col == 1)
                def _():
                    side_copy(0, even, hh).wait_recv()

                    @pl.when(r == 3)
                    def _():
                        up_copy(1, even, hh).wait_recv()

                        @pl.when(climbs)
                        def _():
                            up_copy(1, even, hh).start()

                @pl.when(col == 0)
                def _():
                    side_copy(0, odd, hh).wait_recv()
                    side_copy(1, odd, hh).wait_recv()

                    @pl.when(jnp.logical_not(climbs))
                    def _():
                        side_copy(1, even, hh).wait_recv()
            for kv in range(2):
                for n, b in enumerate((odd, even)):
                    for h, part in enumerate(to_heads(far[kv, hh, b].astype(F32), tmp, share)):
                        fk[kv, hh * share + h, pl.ds((2 * spot + n) * own, own), :] = part

        def body(g, _):
            for n in range(together * (rows // QUAD)):
                h, qd = g * together + n // (rows // QUAD), n % (rows // QUAD)
                at = qd * QUAD
                s = scores(h, at, QUAD, fk[0, h]) + hides[min(qd, 1)]
                merge(h, at, QUAD, s, fk[1, h], 3.0)
            return 0

        for hh in range(together):
            fetch(lower, hh, 0)
            fetch(upper, hh, 1)
            lax.fori_loop(hh * (groups // together), (hh + 1) * (groups // together), body, 0)

    def climb(kv, b, side=None):
        for hh in range(together):
            up_copy(kv, b, hh).wait_recv()

            @pl.when(climbs)
            def _():
                up_copy(kv, b, hh).start()
            if side is not None:
                side_copy(kv, b, hh).start()

    def odd_turn(n):
        def at(turn, r):
            return (n == turn) & (r <= lev)

        @pl.when(n == 1)
        def _():
            climb(1, me - 1)

        for turn, r in ((1, 1), (4, 2), (6, 3)):
            @pl.when(at(turn, r))
            def _():
                climb(0, me - 2 * r, True)

        for turn, r in ((2, 1), (5, 2), (6, 3)):
            @pl.when(at(turn, r))
            def _():
                climb(1, me - 2 * r, True)

        for turn, r in ((3, 1), (5, 2)):
            @pl.when(at(turn, r))
            def _():
                climb(1, me - 2 * r - 1)
                if r == 1:
                    @pl.when(jnp.logical_not(climbs))
                    def _():
                        every(side_copy, 1, me - 3, "start")

        @pl.when((n >= 8) & (n - 4 <= lev))
        def _():
            b = me - 2 * (n - 4)
            for kv in range(2):
                climb(kv, b, True)
            climb(1, b - 1)

    def even_turn(n):
        def relay(kv, part):
            @pl.when(climbs)
            def _():
                thru_copy(kv, part).wait_recv()
                relay_copy(kv, part).start()

        def cross(r):
            @pl.when(r <= lev)
            def _():
                climb(0, me - 2 * r, True)

        def rise(r):
            @pl.when((r <= lev) & climbs)
            def _():
                climb(1, me - 2 * r)

        @pl.when(n == 1)
        def _():
            cross(1)
            tail_copy(0, 0).start()
            tail_copy(0, 1).start()
            relay(0, 0)

        @pl.when(n == 2)
        def _():
            relay(0, 1)
            rise(1)

        @pl.when(n == 3)
        def _():
            cross(2)
            tail_copy(1, 0).start()
            tail_copy(1, 1).start()

        @pl.when(n == 4)
        def _():
            relay(1, 0)
            relay(1, 1)
            rise(2)

        @pl.when(n == 5)
        def _():
            cross(3)

        @pl.when(n == 7)
        def _():
            rise(3)

        @pl.when(n >= 8)
        def _():
            cross(n - 4)
            rise(n - 4)

    def turn(n, _):
        @pl.when(col == 1)
        def _():
            odd_turn(n)

        @pl.when(col == 0)
        def _():
            even_turn(n)

        first = jnp.where(lax.rem(n, 2) == 0, 0, early)
        count = jnp.where(lax.rem(n, 2) == 0, early, groups - early)

        @pl.when(n < 2)
        def _():
            nearest(first, count)

        @pl.when(n == 2)
        def _():
            extra()

        @pl.when((n == 2) | (n == 3))
        def _():
            for qd in range(1, rows // QUAD):
                near(qd, first, count)

        @pl.when((n == 6) & (me > 0))
        def _():
            previous()

        lower = jnp.where(n < 6, 1, ((n - 5) // 2) * 2 + 1)
        ready = (n == 5) | (n >= 7) & ((lax.rem(n, 2) == 0) | (n - 4 == lev))

        @pl.when(ready & (lower <= lev))
        def _():
            distant(lower)
        return 0

    lax.fori_loop(0, jnp.maximum(6, lev + 4) + 1, turn, 0)

    for c in range(rows // HALF):
        for h in range(heads):
            otmp[pl.ds(h, HALF, stride=heads), :] = (
                acc[h, pl.ds(c * HALF, HALF), :] / total[h, pl.ds(c * HALF, HALF), :])
        o_ref[pl.ds(c * HALF, HALF)] = otmp[...].reshape(HALF, heads, width).astype(BF16)

    @pl.when(col == 0)
    def _():
        every(side_copy, 1, me, "wait_send")
        every(side_copy, 0, me, "wait_send")
        for kv in range(2):
            for part in range(2):
                tail_copy(kv, part).wait_send()

        @pl.when(climbs)
        def _():
            every(up_copy, 0, me, "wait_send")
            for kv in range(2):
                for part in range(2):
                    relay_copy(kv, part).wait_send()

        @pl.when(lev < levels - 2)
        def _():
            every(up_copy, 1, me, "wait_send")

    @pl.when((col == 1) & climbs)
    def _():
        every(up_copy, 0, me, "wait_send")
        every(up_copy, 1, me, "wait_send")
        every(up_copy, 1, me - 1, "wait_send")
        for kv in range(2):
            for part in range(2):
                thru_copy(kv, part).wait_send()

    def sent(r, _):
        b = me - 2 * r
        every(side_copy, 0, b, "wait_send")

        @pl.when(climbs)
        def _():
            every(up_copy, 0, b, "wait_send")
            every(up_copy, 1, b, "wait_send")

        @pl.when(col == 1)
        def _():
            every(side_copy, 1, b, "wait_send")

            @pl.when(climbs)
            def _():
                every(up_copy, 1, b - 1, "wait_send")

            @pl.when((r == 1) & jnp.logical_not(climbs))
            def _():
                every(side_copy, 1, b - 1, "wait_send")
        return 0

    lax.fori_loop(1, lev + 1, sent, 0)


def shards(size, queries, keys, values):
    rows, heads, width = queries.shape
    own = rows // 8
    parts = 2 - heads % 2
    vmem = pl.BlockSpec(memory_space=pltpu.VMEM)
    return pl.pallas_call(
        functools.partial(kernel, size),
        out_shape=pltpu.VMEM((rows, heads, width), BF16),
        in_specs=[pl.BlockSpec(memory_space=pl.ANY)] * 3,
        out_specs=vmem,
        scratch_shapes=[
            pltpu.VMEM((rows, heads, width), BF16),
            pltpu.VMEM((rows, heads, width), BF16),
            pltpu.VMEM((rows, heads, width), BF16),
            pltpu.VMEM((2, parts, size, own, heads // parts, width), BF16),
            pltpu.VMEM((2, 2, BLOCK, heads, width), BF16),
            pltpu.VMEM((2, 2, BLOCK, heads, width), BF16),
            pltpu.VMEM((2, BLOCK, heads, width), BF16),
            pltpu.VMEM((heads, rows, width), BF16),
            pltpu.VMEM((2, heads, rows, width), BF16),
            pltpu.VMEM((2, heads, rows // 2 - BLOCK, width), BF16),
            pltpu.VMEM((2, heads, rows // 4 - BLOCK, width), BF16),
            pltpu.VMEM((2, heads, QUAD, width), BF16),
            pltpu.VMEM((2, heads, 4 * own, width), BF16),
            pltpu.VMEM((2, HALF, NEAR), F32),
            pltpu.VMEM((HALF, 3 * HALF), F32),
            pltpu.VMEM((HALF, 3 * HALF), F32),
            pltpu.VMEM((heads, rows, width), F32),
            pltpu.VMEM((heads, rows, width), F32),
            pltpu.VMEM((heads, rows, width), F32),
            pltpu.VMEM((80 * heads, width), F32),
            pltpu.VMEM((HALF * heads, width), F32),
            pltpu.SemaphoreType.DMA((3,)),
            pltpu.SemaphoreType.DMA((2, parts, size)),
            pltpu.SemaphoreType.DMA((2, parts, size)),
            pltpu.SemaphoreType.DMA((2, parts, size)),
            pltpu.SemaphoreType.DMA((2, 2)),
            pltpu.SemaphoreType.DMA((2, 2)),
            pltpu.SemaphoreType.DMA((2, 2)),
            pltpu.SemaphoreType.DMA((2, 2)),
        ],
        compiler_params=pltpu.CompilerParams(
            collective_id=0, has_side_effects=True, vmem_limit_bytes=60 * 2**20),
    )(queries, keys, values)


def solution(mesh):
    spec = P(("groups", "seq"), "heads", None)
    return jax.shard_map(
        functools.partial(shards, mesh.shape["seq"]),
        mesh=mesh, in_specs=(spec,) * 3, out_specs=spec, check_vma=False)
```

```python
import functools
import math

import jax
import jax.numpy as jnp
from jax import lax
from jax.experimental import pallas as pl
from jax.experimental.pallas import tpu as pltpu
from jax.sharding import PartitionSpec as P

BLOCK = 64
QUAD = 4 * BLOCK
HALF = 2 * BLOCK
NEAR = 6 * BLOCK
NEG = -1e30
F32 = jnp.float32
BF16 = jnp.bfloat16


def to_heads(values, scratch, heads):
    count, _, width = values.shape
    scratch[pl.ds(0, count * heads), :] = values.reshape(count * heads, width)
    return [scratch[pl.ds(h, count, stride=heads), :].astype(BF16) for h in range(heads)]


def halved(values):
    count, heads, width = values.shape
    pairs = values.reshape(count // 2, 2, heads, width)
    return pairs[:, 0] + pairs[:, 1]


def across(column, count):
    width = column.shape[1]
    return jnp.concatenate([column] * (count // width), 1) if count > width else column


def with_ones(values):
    return jnp.concatenate([values, jnp.ones_like(values)], 1)


def kernel(size, q_hbm, k_hbm, v_hbm, o_ref,
           q_ref, k_ref, v_ref, far, tail, thru, sendp, eq, e0, e1, e2, before, fk,
           mask1, mask0, maskt, acc, top, total, tmp, otmp,
           in_sem, recv, up_send, side_send, t_send, t_recv, r_send, r_recv):
    rows, heads, width = q_ref.shape
    own = rows // 8
    blocks = rows // BLOCK
    gain = math.log2(math.e) / math.sqrt(width)
    me = lax.axis_index("seq")
    col = lax.rem(me, 2)
    lev = me // 2
    levels = size // 2
    together = 2 - heads % 2
    groups = heads // together
    early = (groups + 1) // 2
    share = heads // together
    climbs = lev < levels - 1
    pair = me + 1 - 2 * col
    up = jnp.minimum(me + 2, size - 1)
    sources = (k_ref, v_ref)

    def remote(src, dst, send, got, target):
        return pltpu.make_async_remote_copy(
            src_ref=src, dst_ref=dst, send_sem=send, recv_sem=got,
            device_id={"seq": target}, device_id_type=pl.DeviceIdType.MESH)

    def up_copy(kv, b, hh):
        place = far.at[kv, hh, b]
        return remote(place, place, up_send.at[kv, hh, b], recv.at[kv, hh, b], up)

    def side_copy(kv, b, hh):
        place = far.at[kv, hh, b]
        return remote(place, place, side_send.at[kv, hh, b], recv.at[kv, hh, b], pair)

    def every(copy, kv, b, action):
        for hh in range(together):
            getattr(copy(kv, b, hh), action)()

    def tail_source(kv, part):
        return sources[kv].at[pl.ds(rows - BLOCK, BLOCK)] if part == 0 else sendp.at[kv]

    def tail_copy(kv, part):
        return remote(tail_source(kv, part), tail.at[kv, part], t_send.at[kv, part], t_recv.at[kv, part], pair)

    def thru_copy(kv, part):
        return remote(tail_source(kv, part), thru.at[kv, part], t_send.at[kv, part], r_recv.at[kv, part], pair)

    def relay_copy(kv, part):
        return remote(thru.at[kv, part], tail.at[kv, part], r_send.at[kv, part], t_recv.at[kv, part], up)

    barrier = pltpu.get_barrier_semaphore()
    for step in (-2, 2):
        @pl.when((me + step >= 0) & (me + step < size))
        def _():
            pl.semaphore_signal(barrier, inc=1, device_id={"seq": me + step},
                                device_id_type=pl.DeviceIdType.MESH)
    pl.semaphore_signal(barrier, inc=1, device_id={"seq": pair}, device_id_type=pl.DeviceIdType.MESH)

    loads = [pltpu.make_async_copy(src, dst, in_sem.at[n]) for n, (src, dst) in enumerate(
        ((v_hbm, v_ref), (k_hbm, k_ref), (q_hbm, q_ref)))]
    for load in loads:
        load.start()

    def split(kv, c):
        x = sources[kv][pl.ds(c * BLOCK, BLOCK)].astype(F32)
        two = halved(x)
        four = halved(two)
        eight = halved(four)
        eight = (eight * 0.125).astype(BF16)
        for hh in range(together):
            far[kv, hh, me, pl.ds(c * 8, 8)] = eight[:, hh * share:(hh + 1) * share]
        if c == blocks - 2:
            sendp[kv, pl.ds(0, 32)] = (two * 0.5).astype(BF16)
        if blocks - 4 <= c < blocks - 2:
            sendp[kv, pl.ds(32 + 16 * (c - blocks + 4), 16)] = (four * 0.25).astype(BF16)

    def spread(kv, c):
        x = sources[kv][pl.ds(c * BLOCK, BLOCK)].astype(F32)
        for h, part in enumerate(to_heads(x, tmp, heads)):
            e0[kv, h, pl.ds(c * BLOCK, BLOCK), :] = part
        if c < blocks - 2:
            two = halved(x)
            for h, part in enumerate(to_heads(two * 0.5, tmp, heads)):
                e1[kv, h, pl.ds(c * 32, 32), :] = part
            if c < blocks - 4:
                four = halved(two)
                for h, part in enumerate(to_heads(four * 0.25, tmp, heads)):
                    e2[kv, h, pl.ds(c * 16, 16), :] = part

    for kv in (1, 0):
        loads[1 - kv].wait()
        for c in range(blocks):
            split(kv, c)

    pl.semaphore_wait(barrier, 1 + jnp.where(lev > 0, 1, 0) + jnp.where(climbs, 1, 0))

    @pl.when(col == 0)
    def _():
        every(side_copy, 1, me, "start")
        every(side_copy, 0, me, "start")

        @pl.when(climbs)
        def _():
            every(up_copy, 0, me, "start")

        for hh in range(together):
            @pl.when(climbs if hh == 0 else lev < levels - 2)
            def _():
                up_copy(1, me, hh).start()

    @pl.when((col == 1) & climbs)
    def _():
        every(up_copy, 0, me, "start")
        every(up_copy, 1, me, "start")
        for kv in range(2):
            for part in range(2):
                thru_copy(kv, part).start()

    for kv in range(2):
        for c in range(blocks):
            spread(kv, c)
    loads[2].wait()
    for c in range(blocks):
        x = q_ref[pl.ds(c * BLOCK, BLOCK)].astype(F32)
        for h, part in enumerate(to_heads(x, tmp, heads)):
            eq[h, pl.ds(c * BLOCK, BLOCK), :] = part

    def grid(count):
        return (lax.broadcasted_iota(jnp.int32, (HALF, count), 0),
                lax.broadcasted_iota(jnp.int32, (HALF, count), 1))

    i, j = grid(NEAR)
    level = jnp.where(j < 192, 0.0, jnp.where(j < 256, 1.0, jnp.where(j < 320, 2.0, 3.0)))
    seen01 = jnp.where(j < 192, jnp.where((j <= i + BLOCK) & ((j >= BLOCK) | (i < BLOCK)), 1, 0),
                       jnp.where((j < 224) | (i >= BLOCK), 1, 0))
    for hf in range(2):
        seen = jnp.where(j < 256, seen01, jnp.where(j < 320, jnp.where((j < 288) | (hf == 1), 1, 0), col))
        mask1[hf] = jnp.where(seen > 0, level, NEG)
    i, j = grid(HALF)
    mask0[:, pl.ds(0, HALF)] = jnp.where(j <= i, 0.0, NEG)
    i, j = grid(2 * HALF)
    seen0 = jnp.where(j < 192, jnp.where((j <= i + BLOCK) & ((j >= BLOCK) | (i < BLOCK)), 1, 0),
                      jnp.where((j < 224) | (i >= BLOCK), 1, 0))
    mask0[:, pl.ds(HALF, 2 * HALF)] = jnp.where(seen0 > 0, jnp.where(j < 192, 0.0, 1.0), NEG)
    ends = jnp.where(j < 192 + own // 2, col, 0)
    level = jnp.where(j < 64, 0.0, jnp.where(j < 128, 1.0, jnp.where(j < 192, 2.0, 3.0)))
    for hf in range(2):
        seent = jnp.where(j < 64, jnp.where(i < BLOCK, 1 - hf, 0),
                          jnp.where(j < 128, jnp.where((j < 96) | (i >= BLOCK), 1 - hf, 0),
                                    jnp.where(j < 192, jnp.where((j < 160) | (hf == 1), 1, 0), ends)))
        maskt[pl.ds(hf * HALF, HALF), :] = jnp.where(seent > 0, level, NEG)

    def begin(h, at, kk, vv, mask):
        s = lax.dot_general(eq[h, pl.ds(at, HALF), :], kk, (((1,), (1,)), ((), ())),
                            preferred_element_type=F32)
        s = s * gain + mask
        m = jnp.broadcast_to(jnp.max(s, axis=1, keepdims=True), (HALF, width))
        w = jnp.exp2(s - across(m, s.shape[1])).astype(BF16)
        both = jnp.dot(w, with_ones(vv), preferred_element_type=F32)
        top[h, pl.ds(at, HALF), :] = m
        acc[h, pl.ds(at, HALF), :] = both[:, :width]
        total[h, pl.ds(at, HALF), :] = both[:, width:]

    def near(qd, first, count):
        def body(g, _):
            for part in range(2 * together):
                h, hf = g * together + part // 2, part % 2
                at = qd * QUAD + hf * HALF
                kk, vv = (jnp.concatenate([
                    e0[kv, h, pl.ds(at - BLOCK, 192), :],
                    e1[kv, h, pl.ds(at // 2 - BLOCK, BLOCK), :],
                    e2[kv, h, pl.ds((qd - 1) * BLOCK, BLOCK), :],
                    before[kv, h, pl.ds(3 * BLOCK, BLOCK)]], 0) for kv in range(2))
                begin(h, at, kk, vv, mask1[hf])
            return 0
        lax.fori_loop(first, first + count, body, 0)

    def nearest(first, count):
        def body(g, _):
            for n in range(together):
                h = g * together + n
                begin(h, 0, e0[0, h, pl.ds(0, HALF), :], e0[1, h, pl.ds(0, HALF), :], mask0[:, pl.ds(0, HALF)])
                kk, vv = (jnp.concatenate([
                    e0[kv, h, pl.ds(BLOCK, 192), :], e1[kv, h, pl.ds(0, BLOCK), :]], 0) for kv in range(2))
                begin(h, HALF, kk, vv, mask0[:, pl.ds(HALF, 2 * HALF)])
            return 0
        lax.fori_loop(first, first + count, body, 0)

    def merge(h, at, count, s, vv, lift):
        m = top[h, pl.ds(at, count), :]
        peak = jnp.max(s, axis=1, keepdims=True)
        if lift is not None:
            peak = peak * gain + lift
            s = s * gain
        fresh = jnp.maximum(m, peak)
        fade = jnp.exp2(m - fresh)
        w = jnp.exp2(s - across(fresh if lift is None else fresh - lift, s.shape[1])).astype(BF16)
        both = jnp.dot(w, with_ones(vv), preferred_element_type=F32)
        top[h, pl.ds(at, count), :] = fresh
        acc[h, pl.ds(at, count), :] = acc[h, pl.ds(at, count), :] * fade + both[:, :width]
        total[h, pl.ds(at, count), :] = total[h, pl.ds(at, count), :] * fade + both[:, width:]

    def scores(h, at, count, kk):
        return lax.dot_general(eq[h, pl.ds(at, count), :], kk, (((1,), (1,)), ((), ())),
                               preferred_element_type=F32)

    def extra():
        @pl.when(col == 1)
        def _():
            every(side_copy, 0, me - 1, "wait_recv")
            for kv in range(2):
                for hh in range(together):
                    for h, part in enumerate(to_heads(far[kv, hh, me - 1].astype(F32), tmp, share)):
                        before[kv, hh * share + h, pl.ds(3 * BLOCK, own)] = part

        @pl.when(col == 0)
        def _():
            for kv in range(2):
                for h in range(heads):
                    before[kv, h, pl.ds(3 * BLOCK, own)] = jnp.zeros((own, width), BF16)

    def previous():
        for kv in range(2):
            for part in range(2):
                tail_copy(kv, part).wait_recv()
            x = tail[kv, 0].astype(F32)
            two = halved(x)
            four = halved(two)
            y = tail[kv, 1].astype(F32)
            late = halved(y[:32])
            for h, part in enumerate(to_heads(x, tmp, heads)):
                before[kv, h, pl.ds(0, BLOCK), :] = part
            for h, part in enumerate(to_heads(two * 0.5, tmp, heads)):
                before[kv, h, pl.ds(96, 32), :] = part
            for h, part in enumerate(to_heads(four * 0.25, tmp, heads)):
                before[kv, h, pl.ds(176, 16), :] = part
            for h, part in enumerate(to_heads(late * 0.5, tmp, heads)):
                before[kv, h, pl.ds(160, 16), :] = part
            for h, part in enumerate(to_heads(y, tmp, heads)):
                before[kv, h, pl.ds(64, 32), :] = part[:32]
                before[kv, h, pl.ds(128, 32), :] = part[32:]

        def body(g, _):
            for n in range(together):
                h = g * together + n
                s = scores(h, 0, QUAD, before[0, h]) * gain + maskt[...]
                merge(h, 0, QUAD, s, before[1, h], None)
            return 0
        lax.fori_loop(0, groups, body, 0)

    def arrange(hh):
        for h in range(hh * share, (hh + 1) * share):
            for c in range(rows // HALF):
                otmp[pl.ds(c * HALF * heads + h, HALF, stride=heads), :] = (
                    acc[h, pl.ds(c * HALF, HALF), :] / total[h, pl.ds(c * HALF, HALF), :])

    def distant(lower, upper, final):
        place = lax.broadcasted_iota(jnp.int32, (1, 4 * own), 1)
        gone = (place >= 2 * own) & (upper == lower)
        inner = (col == 0) & (lower == 1) & (place >= own // 2) & (place < own)
        hides = [jnp.where(gone | inner, NEG, 0.0), jnp.where(gone, NEG, 0.0)]

        def fetch(r, hh, spot):
            odd = me - 2 * r + 1 - col
            even = me - 2 * r - col

            @pl.when((spot == 0) | (upper > lower))
            def _():
                @pl.when(col == 1)
                def _():
                    side_copy(0, even, hh).wait_recv()

                    @pl.when(r == 3)
                    def _():
                        up_copy(1, even, hh).wait_recv()

                        @pl.when(climbs)
                        def _():
                            up_copy(1, even, hh).start()

                    if hh > 0:
                        @pl.when((r == 2) & jnp.logical_not(climbs))
                        def _():
                            up_copy(1, even, hh).wait_recv()

                @pl.when(col == 0)
                def _():
                    side_copy(0, odd, hh).wait_recv()
                    side_copy(1, odd, hh).wait_recv()

                    @pl.when(jnp.logical_not(climbs))
                    def _():
                        side_copy(1, even, hh).wait_recv()
            for kv in range(2):
                for n, b in enumerate((odd, even)):
                    for h, part in enumerate(to_heads(far[kv, hh, b].astype(F32), tmp, share)):
                        fk[kv, hh * share + h, pl.ds((2 * spot + n) * own, own), :] = part

        def body(g, _):
            for n in range(together * (rows // QUAD)):
                h, qd = g * together + n // (rows // QUAD), n % (rows // QUAD)
                at = qd * QUAD
                s = scores(h, at, QUAD, fk[0, h]) + hides[min(qd, 1)]
                merge(h, at, QUAD, s, fk[1, h], 3.0)
            return 0

        for hh in range(together):
            fetch(lower, hh, 0)
            fetch(upper, hh, 1)
            lax.fori_loop(hh * (groups // together), (hh + 1) * (groups // together), body, 0)

            @pl.when(final)
            def _():
                arrange(hh)

    def climb(kv, b, side=None, halves=tuple(range(together))):
        for hh in halves:
            up_copy(kv, b, hh).wait_recv()

            @pl.when(climbs)
            def _():
                up_copy(kv, b, hh).start()
            if side is not None:
                side_copy(kv, b, hh).start()

    def odd_turn(n):
        def at(turn, r):
            return (n == turn) & (r <= lev)

        @pl.when(n == 1)
        def _():
            climb(1, me - 1)

        for turn, r in ((1, 1), (4, 2), (6, 3)):
            @pl.when(at(turn, r))
            def _():
                climb(0, me - 2 * r, True)

        for turn, r in ((2, 1), (5, 2), (6, 3)):
            @pl.when(at(turn, r))
            def _():
                climb(1, me - 2 * r, True)

        @pl.when(at(3, 1))
        def _():
            every(up_copy, 1, me - 3, "wait_recv")

            @pl.when(lev == levels - 1)
            def _():
                for hh in range(1, together):
                    side_copy(1, me - 3, hh).start()

            @pl.when(climbs)
            def _():
                up_copy(1, me - 3, 0).start()

            @pl.when(lev < levels - 2)
            def _():
                for hh in range(1, together):
                    up_copy(1, me - 3, hh).start()

        @pl.when(at(5, 2))
        def _():
            climb(1, me - 5, None, (0,))

            @pl.when(lev == levels - 1)
            def _():
                side_copy(1, me - 5, 0).start()

        @pl.when(at(5, 1) & (lev == levels - 2))
        def _():
            for hh in range(1, together):
                up_copy(1, me - 3, hh).start()

        @pl.when(at(5, 2) & climbs)
        def _():
            for hh in range(1, together):
                climb(1, me - 5, None, (hh,))

        @pl.when((n >= 8) & (n - 4 <= lev))
        def _():
            b = me - 2 * (n - 4)
            for kv in range(2):
                climb(kv, b, True)
            climb(1, b - 1)

    def even_turn(n):
        def relay(kv, part):
            @pl.when(climbs)
            def _():
                thru_copy(kv, part).wait_recv()
                relay_copy(kv, part).start()

        def cross(r):
            @pl.when(r <= lev)
            def _():
                climb(0, me - 2 * r, True)

        def rise(r):
            @pl.when((r <= lev) & climbs)
            def _():
                climb(1, me - 2 * r)

        @pl.when(n == 1)
        def _():
            cross(1)
            for kv in range(2):
                for part in range(2):
                    tail_copy(kv, part).start()
            relay(0, 0)

        @pl.when(n == 2)
        def _():
            relay(0, 1)

            @pl.when((lev >= 1) & climbs)
            def _():
                every(up_copy, 1, me - 2, "wait_recv")

                @pl.when(lev < levels - 2)
                def _():
                    every(up_copy, 1, me - 2, "start")

        @pl.when(n == 3)
        def _():
            cross(2)

        @pl.when(n == 4)
        def _():
            relay(1, 0)
            relay(1, 1)

            @pl.when((lev >= 2) & climbs)
            def _():
                climb(1, me - 4, None, (0,))

            @pl.when((lev >= 1) & (lev == levels - 2))
            def _():
                for hh in range(1, together):
                    up_copy(1, me - 2, hh).start()

            @pl.when((lev >= 2) & climbs)
            def _():
                for hh in range(1, together):
                    climb(1, me - 4, None, (hh,))

        @pl.when(n == 5)
        def _():
            cross(3)

        @pl.when(n == 7)
        def _():
            rise(3)

        @pl.when(n >= 8)
        def _():
            cross(n - 4)
            rise(n - 4)

    def turn(n, _):
        @pl.when(col == 1)
        def _():
            odd_turn(n)

        @pl.when(col == 0)
        def _():
            even_turn(n)

        first = jnp.where(lax.rem(n, 2) == 0, 0, early)
        count = jnp.where(lax.rem(n, 2) == 0, early, groups - early)

        @pl.when(n < 2)
        def _():
            nearest(first, count)

        @pl.when(n == 2)
        def _():
            extra()

        @pl.when((n == 2) | (n == 3))
        def _():
            for qd in range(1, rows // QUAD):
                near(qd, first, count)

        @pl.when((n == 6) & (me > 0))
        def _():
            previous()

        upper = jnp.where(n < 6, n - 3, n - 4)
        lower = jnp.maximum(upper - 1, 1)
        even = lax.rem(lev - upper, 2) == 0

        @pl.when((n >= 4) & (n != 6) & (upper <= lev) & even)
        def _():
            distant(lower, upper, (n >= 7) & (upper == lev))
        return 0

    lax.fori_loop(0, jnp.maximum(6, lev + 4) + 1, turn, 0)

    @pl.when(lev < 3)
    def _():
        for hh in range(together):
            arrange(hh)

    for c in range(rows // HALF):
        o_ref[pl.ds(c * HALF, HALF)] = (
            otmp[pl.ds(c * HALF * heads, HALF * heads), :].reshape(HALF, heads, width).astype(BF16))

    @pl.when(col == 0)
    def _():
        every(side_copy, 1, me, "wait_send")
        every(side_copy, 0, me, "wait_send")
        for kv in range(2):
            for part in range(2):
                tail_copy(kv, part).wait_send()

        @pl.when(climbs)
        def _():
            every(up_copy, 0, me, "wait_send")
            for kv in range(2):
                for part in range(2):
                    relay_copy(kv, part).wait_send()

        for hh in range(together):
            @pl.when(climbs if hh == 0 else lev < levels - 2)
            def _():
                up_copy(1, me, hh).wait_send()

    @pl.when((col == 1) & climbs)
    def _():
        every(up_copy, 0, me, "wait_send")
        every(up_copy, 1, me, "wait_send")
        every(up_copy, 1, me - 1, "wait_send")
        for kv in range(2):
            for part in range(2):
                thru_copy(kv, part).wait_send()

    def sent(r, _):
        b = me - 2 * r
        every(side_copy, 0, b, "wait_send")

        @pl.when(climbs)
        def _():
            every(up_copy, 0, b, "wait_send")

            for hh in range(together):
                @pl.when((hh > 0) | (col == 1) | (r > 1) | (lev < levels - 2))
                def _():
                    up_copy(1, b, hh).wait_send()

        @pl.when(col == 1)
        def _():
            every(side_copy, 1, b, "wait_send")

            @pl.when(climbs)
            def _():
                every(up_copy, 1, b - 1, "wait_send")

            for hh in range(together):
                @pl.when((r == (2 if hh == 0 else 1)) & jnp.logical_not(climbs))
                def _():
                    side_copy(1, b - 1, hh).wait_send()
        return 0

    lax.fori_loop(1, lev + 1, sent, 0)


def shards(size, queries, keys, values):
    rows, heads, width = queries.shape
    own = rows // 8
    parts = 2 - heads % 2
    vmem = pl.BlockSpec(memory_space=pltpu.VMEM)
    return pl.pallas_call(
        functools.partial(kernel, size),
        out_shape=pltpu.VMEM((rows, heads, width), BF16),
        in_specs=[pl.BlockSpec(memory_space=pl.ANY)] * 3,
        out_specs=vmem,
        scratch_shapes=[
            pltpu.VMEM((rows, heads, width), BF16),
            pltpu.VMEM((rows, heads, width), BF16),
            pltpu.VMEM((rows, heads, width), BF16),
            pltpu.VMEM((2, parts, size, own, heads // parts, width), BF16),
            pltpu.VMEM((2, 2, BLOCK, heads, width), BF16),
            pltpu.VMEM((2, 2, BLOCK, heads, width), BF16),
            pltpu.VMEM((2, BLOCK, heads, width), BF16),
            pltpu.VMEM((heads, rows, width), BF16),
            pltpu.VMEM((2, heads, rows, width), BF16),
            pltpu.VMEM((2, heads, rows // 2 - BLOCK, width), BF16),
            pltpu.VMEM((2, heads, rows // 4 - BLOCK, width), BF16),
            pltpu.VMEM((2, heads, QUAD, width), BF16),
            pltpu.VMEM((2, heads, 4 * own, width), BF16),
            pltpu.VMEM((2, HALF, NEAR), F32),
            pltpu.VMEM((HALF, 3 * HALF), F32),
            pltpu.VMEM((QUAD, QUAD), F32),
            pltpu.VMEM((heads, rows, width), F32),
            pltpu.VMEM((heads, rows, width), F32),
            pltpu.VMEM((heads, rows, width), F32),
            pltpu.VMEM((80 * heads, width), F32),
            pltpu.VMEM((rows * heads, width), F32),
            pltpu.SemaphoreType.DMA((3,)),
            pltpu.SemaphoreType.DMA((2, parts, size)),
            pltpu.SemaphoreType.DMA((2, parts, size)),
            pltpu.SemaphoreType.DMA((2, parts, size)),
            pltpu.SemaphoreType.DMA((2, 2)),
            pltpu.SemaphoreType.DMA((2, 2)),
            pltpu.SemaphoreType.DMA((2, 2)),
            pltpu.SemaphoreType.DMA((2, 2)),
        ],
        compiler_params=pltpu.CompilerParams(
            collective_id=0, has_side_effects=True, vmem_limit_bytes=60 * 2**20),
    )(queries, keys, values)


def solution(mesh):
    spec = P(("groups", "seq"), "heads", None)
    return jax.shard_map(
        functools.partial(shards, mesh.shape["seq"]),
        mesh=mesh, in_specs=(spec,) * 3, out_specs=spec, check_vma=False)
```

```python
import functools
import math

import jax
import jax.numpy as jnp
from jax import lax
from jax.experimental import pallas as pl
from jax.experimental.pallas import tpu as pltpu
from jax.sharding import PartitionSpec as P

BLOCK = 64
QUAD = 4 * BLOCK
HALF = 2 * BLOCK
NEAR = 6 * BLOCK
NEG = -1e30
F32 = jnp.float32
BF16 = jnp.bfloat16


def to_heads(values, scratch, heads):
    count, _, width = values.shape
    scratch[pl.ds(0, count * heads), :] = values.reshape(count * heads, width)
    return [scratch[pl.ds(h, count, stride=heads), :].astype(BF16) for h in range(heads)]


def halved(values):
    count, heads, width = values.shape
    pairs = values.reshape(count // 2, 2, heads, width)
    return pairs[:, 0] + pairs[:, 1]


def across(column, count):
    width = column.shape[1]
    return jnp.concatenate([column] * (count // width), 1) if count > width else column


def with_ones(values):
    return jnp.concatenate([values, jnp.ones_like(values)], 1)


def kernel(size, q_hbm, k_hbm, v_hbm, o_ref,
           q_ref, k_ref, v_ref, far, tail, thru, sendp, eq, e0, e1, e2, before, fk,
           mask1, mask0, maskt, acc, top, total, tmp, otmp,
           in_sem, recv, up_send, side_send, t_send, t_recv, r_send, r_recv):
    rows, heads, width = q_ref.shape
    own = rows // 8
    blocks = rows // BLOCK
    gain = math.log2(math.e) / math.sqrt(width)
    me = lax.axis_index("seq")
    col = lax.rem(me, 2)
    lev = me // 2
    levels = size // 2
    together = 2 - heads % 2
    groups = heads // together
    early = (groups + 1) // 2
    share = heads // together
    climbs = lev < levels - 1
    pair = me + 1 - 2 * col
    up = jnp.minimum(me + 2, size - 1)
    sources = (k_ref, v_ref)

    def remote(src, dst, send, got, target):
        return pltpu.make_async_remote_copy(
            src_ref=src, dst_ref=dst, send_sem=send, recv_sem=got,
            device_id={"seq": target}, device_id_type=pl.DeviceIdType.MESH)

    def up_copy(kv, b, hh):
        place = far.at[kv, hh, b]
        return remote(place, place, up_send.at[kv, hh, b], recv.at[kv, hh, b], up)

    def side_copy(kv, b, hh):
        place = far.at[kv, hh, b]
        return remote(place, place, side_send.at[kv, hh, b], recv.at[kv, hh, b], pair)

    def every(copy, kv, b, action):
        for hh in range(together):
            getattr(copy(kv, b, hh), action)()

    def tail_source(kv, part):
        return sources[kv].at[pl.ds(rows - BLOCK, BLOCK)] if part == 0 else sendp.at[kv]

    def tail_copy(kv, part):
        return remote(tail_source(kv, part), tail.at[kv, part], t_send.at[kv, part], t_recv.at[kv, part], pair)

    def thru_copy(kv, part):
        return remote(tail_source(kv, part), thru.at[kv, part], t_send.at[kv, part], r_recv.at[kv, part], pair)

    def relay_copy(kv, part):
        return remote(thru.at[kv, part], tail.at[kv, part], r_send.at[kv, part], t_recv.at[kv, part], up)

    barrier = pltpu.get_barrier_semaphore()
    for step in (-2, 2):
        @pl.when((me + step >= 0) & (me + step < size))
        def _():
            pl.semaphore_signal(barrier, inc=1, device_id={"seq": me + step},
                                device_id_type=pl.DeviceIdType.MESH)
    pl.semaphore_signal(barrier, inc=1, device_id={"seq": pair}, device_id_type=pl.DeviceIdType.MESH)

    loads = [pltpu.make_async_copy(src, dst, in_sem.at[n]) for n, (src, dst) in enumerate(
        ((v_hbm, v_ref), (k_hbm, k_ref), (q_hbm, q_ref)))]
    for load in loads:
        load.start()

    def split(kv, c):
        x = sources[kv][pl.ds(c * BLOCK, BLOCK)].astype(F32)
        two = halved(x)
        four = halved(two)
        eight = halved(four)
        eight = (eight * 0.125).astype(BF16)
        for hh in range(together):
            far[kv, hh, me, pl.ds(c * 8, 8)] = eight[:, hh * share:(hh + 1) * share]
        if c == blocks - 2:
            sendp[kv, pl.ds(0, 32)] = (two * 0.5).astype(BF16)
        if blocks - 4 <= c < blocks - 2:
            sendp[kv, pl.ds(32 + 16 * (c - blocks + 4), 16)] = (four * 0.25).astype(BF16)

    def spread(kv, c):
        x = sources[kv][pl.ds(c * BLOCK, BLOCK)].astype(F32)
        for h, part in enumerate(to_heads(x, tmp, heads)):
            e0[kv, h, pl.ds(c * BLOCK, BLOCK), :] = part
        if c < blocks - 2:
            two = halved(x)
            for h, part in enumerate(to_heads(two * 0.5, tmp, heads)):
                e1[kv, h, pl.ds(c * 32, 32), :] = part
            if c < blocks - 4:
                four = halved(two)
                for h, part in enumerate(to_heads(four * 0.25, tmp, heads)):
                    e2[kv, h, pl.ds(c * 16, 16), :] = part

    for kv in (1, 0):
        loads[1 - kv].wait()
        for c in range(blocks):
            split(kv, c)

    pl.semaphore_wait(barrier, 1 + jnp.where(lev > 0, 1, 0) + jnp.where(climbs, 1, 0))

    @pl.when(col == 0)
    def _():
        every(side_copy, 1, me, "start")
        every(side_copy, 0, me, "start")

        @pl.when(climbs)
        def _():
            every(up_copy, 0, me, "start")

        for hh in range(together):
            @pl.when(climbs if hh == 0 else lev < levels - 2)
            def _():
                up_copy(1, me, hh).start()

    @pl.when((col == 1) & climbs)
    def _():
        every(up_copy, 0, me, "start")
        every(up_copy, 1, me, "start")
        for kv in range(2):
            for part in range(2):
                thru_copy(kv, part).start()

    for kv in range(2):
        for c in range(blocks):
            spread(kv, c)
    loads[2].wait()
    for c in range(blocks):
        x = q_ref[pl.ds(c * BLOCK, BLOCK)].astype(F32)
        for h, part in enumerate(to_heads(x, tmp, heads)):
            eq[h, pl.ds(c * BLOCK, BLOCK), :] = part

    def grid(count):
        return (lax.broadcasted_iota(jnp.int32, (HALF, count), 0),
                lax.broadcasted_iota(jnp.int32, (HALF, count), 1))

    i, j = grid(NEAR)
    level = jnp.where(j < 192, 0.0, jnp.where(j < 256, 1.0, jnp.where(j < 320, 2.0, 3.0)))
    seen01 = jnp.where(j < 192, jnp.where((j <= i + BLOCK) & ((j >= BLOCK) | (i < BLOCK)), 1, 0),
                       jnp.where((j < 224) | (i >= BLOCK), 1, 0))
    for hf in range(2):
        seen = jnp.where(j < 256, seen01, jnp.where(j < 320, jnp.where((j < 288) | (hf == 1), 1, 0), col))
        mask1[hf] = jnp.where(seen > 0, level, NEG)
    i, j = grid(HALF)
    mask0[:, pl.ds(0, HALF)] = jnp.where(j <= i, 0.0, NEG)
    i, j = grid(2 * HALF)
    seen0 = jnp.where(j < 192, jnp.where((j <= i + BLOCK) & ((j >= BLOCK) | (i < BLOCK)), 1, 0),
                      jnp.where((j < 224) | (i >= BLOCK), 1, 0))
    mask0[:, pl.ds(HALF, 2 * HALF)] = jnp.where(seen0 > 0, jnp.where(j < 192, 0.0, 1.0), NEG)
    ends = jnp.where(j < 192 + own // 2, col, 0)
    level = jnp.where(j < 64, 0.0, jnp.where(j < 128, 1.0, jnp.where(j < 192, 2.0, 3.0)))
    for hf in range(2):
        seent = jnp.where(j < 64, jnp.where(i < BLOCK, 1 - hf, 0),
                          jnp.where(j < 128, jnp.where((j < 96) | (i >= BLOCK), 1 - hf, 0),
                                    jnp.where(j < 192, jnp.where((j < 160) | (hf == 1), 1, 0), ends)))
        maskt[pl.ds(hf * HALF, HALF), :] = jnp.where(seent > 0, level, NEG)

    def begin(h, at, kk, vv, mask):
        s = lax.dot_general(eq[h, pl.ds(at, HALF), :], kk, (((1,), (1,)), ((), ())),
                            preferred_element_type=F32)
        s = s * gain + mask
        m = jnp.broadcast_to(jnp.max(s, axis=1, keepdims=True), (HALF, width))
        w = jnp.exp2(s - across(m, s.shape[1])).astype(BF16)
        both = jnp.dot(w, with_ones(vv), preferred_element_type=F32)
        top[h, pl.ds(at, HALF), :] = m
        acc[h, pl.ds(at, HALF), :] = both[:, :width]
        total[h, pl.ds(at, HALF), :] = both[:, width:]

    def near(qd, first, count):
        def body(g, _):
            for part in range(2 * together):
                h, hf = g * together + part // 2, part % 2
                at = qd * QUAD + hf * HALF
                kk, vv = (jnp.concatenate([
                    e0[kv, h, pl.ds(at - BLOCK, 192), :],
                    e1[kv, h, pl.ds(at // 2 - BLOCK, BLOCK), :],
                    e2[kv, h, pl.ds((qd - 1) * BLOCK, BLOCK), :],
                    before[kv, h, pl.ds(3 * BLOCK, BLOCK)]], 0) for kv in range(2))
                begin(h, at, kk, vv, mask1[hf])
            return 0
        lax.fori_loop(first, first + count, body, 0)

    def nearest(first, count):
        def body(g, _):
            for n in range(together):
                h = g * together + n
                begin(h, 0, e0[0, h, pl.ds(0, HALF), :], e0[1, h, pl.ds(0, HALF), :], mask0[:, pl.ds(0, HALF)])
                kk, vv = (jnp.concatenate([
                    e0[kv, h, pl.ds(BLOCK, 192), :], e1[kv, h, pl.ds(0, BLOCK), :]], 0) for kv in range(2))
                begin(h, HALF, kk, vv, mask0[:, pl.ds(HALF, 2 * HALF)])
            return 0
        lax.fori_loop(first, first + count, body, 0)

    def merge(h, at, count, s, vv, lift):
        m = top[h, pl.ds(at, count), :]
        peak = jnp.max(s, axis=1, keepdims=True)
        if lift is not None:
            peak = peak * gain + lift
            s = s * gain
        fresh = jnp.maximum(m, peak)
        fade = jnp.exp2(m - fresh)
        w = jnp.exp2(s - across(fresh if lift is None else fresh - lift, s.shape[1])).astype(BF16)
        both = jnp.dot(w, with_ones(vv), preferred_element_type=F32)
        top[h, pl.ds(at, count), :] = fresh
        acc[h, pl.ds(at, count), :] = acc[h, pl.ds(at, count), :] * fade + both[:, :width]
        total[h, pl.ds(at, count), :] = total[h, pl.ds(at, count), :] * fade + both[:, width:]

    def scores(h, at, count, kk):
        return lax.dot_general(eq[h, pl.ds(at, count), :], kk, (((1,), (1,)), ((), ())),
                               preferred_element_type=F32)

    def extra():
        @pl.when(col == 1)
        def _():
            every(side_copy, 0, me - 1, "wait_recv")
            for kv in range(2):
                for hh in range(together):
                    for h, part in enumerate(to_heads(far[kv, hh, me - 1].astype(F32), tmp, share)):
                        before[kv, hh * share + h, pl.ds(3 * BLOCK, own)] = part

        @pl.when(col == 0)
        def _():
            for kv in range(2):
                for h in range(heads):
                    before[kv, h, pl.ds(3 * BLOCK, own)] = jnp.zeros((own, width), BF16)

    def previous():
        for kv in range(2):
            for part in range(2):
                tail_copy(kv, part).wait_recv()
            x = tail[kv, 0].astype(F32)
            two = halved(x)
            four = halved(two)
            y = tail[kv, 1].astype(F32)
            late = halved(y[:32])
            for h, part in enumerate(to_heads(x, tmp, heads)):
                before[kv, h, pl.ds(0, BLOCK), :] = part
            for h, part in enumerate(to_heads(two * 0.5, tmp, heads)):
                before[kv, h, pl.ds(96, 32), :] = part
            for h, part in enumerate(to_heads(four * 0.25, tmp, heads)):
                before[kv, h, pl.ds(176, 16), :] = part
            for h, part in enumerate(to_heads(late * 0.5, tmp, heads)):
                before[kv, h, pl.ds(160, 16), :] = part
            for h, part in enumerate(to_heads(y, tmp, heads)):
                before[kv, h, pl.ds(64, 32), :] = part[:32]
                before[kv, h, pl.ds(128, 32), :] = part[32:]

        def body(g, _):
            for n in range(share):
                h = g * share + n
                s = scores(h, 0, QUAD, before[0, h]) * gain + maskt[...]
                merge(h, 0, QUAD, s, before[1, h], None)
            return 0
        lax.fori_loop(0, together, body, 0)

    def arrange(hh):
        for h in range(hh * share, (hh + 1) * share):
            for c in range(rows // HALF):
                otmp[pl.ds(c * HALF * heads + h, HALF, stride=heads), :] = (
                    acc[h, pl.ds(c * HALF, HALF), :] / total[h, pl.ds(c * HALF, HALF), :])

    def distant(lower, upper, final):
        place = lax.broadcasted_iota(jnp.int32, (1, 4 * own), 1)
        gone = (place >= 2 * own) & (upper == lower)
        inner = (col == 0) & (lower == 1) & (place >= own // 2) & (place < own)
        hides = [jnp.where(gone | inner, NEG, 0.0), jnp.where(gone, NEG, 0.0)]

        def fetch(r, hh, spot):
            odd = me - 2 * r + 1 - col
            even = me - 2 * r - col

            @pl.when((spot == 0) | (upper > lower))
            def _():
                @pl.when(col == 1)
                def _():
                    side_copy(0, even, hh).wait_recv()

                    @pl.when(r == 3)
                    def _():
                        up_copy(1, even, hh).wait_recv()

                        @pl.when(climbs)
                        def _():
                            up_copy(1, even, hh).start()

                    if hh > 0:
                        @pl.when((r == 2) & jnp.logical_not(climbs))
                        def _():
                            up_copy(1, even, hh).wait_recv()

                @pl.when(col == 0)
                def _():
                    side_copy(0, odd, hh).wait_recv()
                    side_copy(1, odd, hh).wait_recv()

                    @pl.when(jnp.logical_not(climbs))
                    def _():
                        side_copy(1, even, hh).wait_recv()
            for kv in range(2):
                for n, b in enumerate((odd, even)):
                    for h, part in enumerate(to_heads(far[kv, hh, b].astype(F32), tmp, share)):
                        fk[kv, hh * share + h, pl.ds((2 * spot + n) * own, own), :] = part

        def body(g, _):
            for n in range(share * (rows // QUAD)):
                h, qd = g * share + n // (rows // QUAD), n % (rows // QUAD)
                at = qd * QUAD
                s = scores(h, at, QUAD, fk[0, h]) + hides[min(qd, 1)]
                merge(h, at, QUAD, s, fk[1, h], 3.0)
            return 0

        for hh in range(together):
            fetch(lower, hh, 0)
            fetch(upper, hh, 1)
            lax.fori_loop(hh, hh + 1, body, 0)

            @pl.when(final)
            def _():
                arrange(hh)

    def climb(kv, b, side=None, halves=tuple(range(together))):
        for hh in halves:
            up_copy(kv, b, hh).wait_recv()

            @pl.when(climbs)
            def _():
                up_copy(kv, b, hh).start()
            if side is not None:
                side_copy(kv, b, hh).start()

    def odd_turn(n):
        def at(turn, r):
            return (n == turn) & (r <= lev)

        @pl.when(n == 1)
        def _():
            climb(1, me - 1)

        for turn, r in ((1, 1), (4, 2), (6, 3)):
            @pl.when(at(turn, r))
            def _():
                climb(0, me - 2 * r, True)

        for turn, r in ((2, 1), (5, 2), (6, 3)):
            @pl.when(at(turn, r))
            def _():
                climb(1, me - 2 * r, True)

        @pl.when(at(3, 1))
        def _():
            every(up_copy, 1, me - 3, "wait_recv")

            @pl.when(lev == levels - 1)
            def _():
                for hh in range(1, together):
                    side_copy(1, me - 3, hh).start()

            @pl.when(climbs)
            def _():
                up_copy(1, me - 3, 0).start()

            @pl.when(lev < levels - 2)
            def _():
                for hh in range(1, together):
                    up_copy(1, me - 3, hh).start()

        @pl.when(at(5, 2))
        def _():
            climb(1, me - 5, None, (0,))

            @pl.when(lev == levels - 1)
            def _():
                side_copy(1, me - 5, 0).start()

        @pl.when(at(5, 1) & (lev == levels - 2))
        def _():
            for hh in range(1, together):
                up_copy(1, me - 3, hh).start()

        @pl.when(at(5, 2) & climbs)
        def _():
            for hh in range(1, together):
                climb(1, me - 5, None, (hh,))

        @pl.when((n >= 8) & (n - 4 <= lev))
        def _():
            b = me - 2 * (n - 4)
            for kv in range(2):
                climb(kv, b, True)
            climb(1, b - 1)

    def even_turn(n):
        def relay(kv, part):
            @pl.when(climbs)
            def _():
                thru_copy(kv, part).wait_recv()
                relay_copy(kv, part).start()

        def cross(r):
            @pl.when(r <= lev)
            def _():
                climb(0, me - 2 * r, True)

        def rise(r):
            @pl.when((r <= lev) & climbs)
            def _():
                climb(1, me - 2 * r)

        @pl.when(n == 1)
        def _():
            cross(1)
            for kv in range(2):
                for part in range(2):
                    tail_copy(kv, part).start()
            relay(0, 0)

        @pl.when(n == 2)
        def _():
            relay(0, 1)

            @pl.when((lev >= 1) & climbs)
            def _():
                every(up_copy, 1, me - 2, "wait_recv")

                @pl.when(lev < levels - 2)
                def _():
                    every(up_copy, 1, me - 2, "start")

        @pl.when(n == 3)
        def _():
            cross(2)

        @pl.when(n == 4)
        def _():
            relay(1, 0)
            relay(1, 1)

            @pl.when((lev >= 2) & climbs)
            def _():
                climb(1, me - 4, None, (0,))

            @pl.when((lev >= 1) & (lev == levels - 2))
            def _():
                for hh in range(1, together):
                    up_copy(1, me - 2, hh).start()

            @pl.when((lev >= 2) & climbs)
            def _():
                for hh in range(1, together):
                    climb(1, me - 4, None, (hh,))

        @pl.when(n == 5)
        def _():
            cross(3)

        @pl.when(n == 7)
        def _():
            rise(3)

        @pl.when(n >= 8)
        def _():
            cross(n - 4)
            rise(n - 4)

    def turn(n, _):
        @pl.when(col == 1)
        def _():
            odd_turn(n)

        @pl.when(col == 0)
        def _():
            even_turn(n)

        first = jnp.where(lax.rem(n, 2) == 0, 0, early)
        count = jnp.where(lax.rem(n, 2) == 0, early, groups - early)

        @pl.when(n < 2)
        def _():
            nearest(first, count)

        @pl.when(n == 2)
        def _():
            extra()

        @pl.when((n == 2) | (n == 3))
        def _():
            for qd in range(1, rows // QUAD):
                near(qd, first, count)

        @pl.when((n == jnp.where(lev == 2, 5, 6)) & (me > 0))
        def _():
            previous()

        upper = jnp.where(n < 6, n - 3, n - 4)
        lower = jnp.maximum(upper - 1, 1)
        even = lax.rem(lev - upper, 2) == 0

        @pl.when((n >= 4) & (n != 6) & (upper <= lev) & even)
        def _():
            distant(lower, upper, (n >= 7) & (upper == lev))
        return 0

    lax.fori_loop(0, jnp.maximum(6, lev + 4) + 1, turn, 0)

    @pl.when(lev < 3)
    def _():
        for hh in range(together):
            arrange(hh)

    for c in range(rows // HALF):
        o_ref[pl.ds(c * HALF, HALF)] = (
            otmp[pl.ds(c * HALF * heads, HALF * heads), :].reshape(HALF, heads, width).astype(BF16))

    @pl.when(col == 0)
    def _():
        every(side_copy, 1, me, "wait_send")
        every(side_copy, 0, me, "wait_send")
        for kv in range(2):
            for part in range(2):
                tail_copy(kv, part).wait_send()

        @pl.when(climbs)
        def _():
            every(up_copy, 0, me, "wait_send")
            for kv in range(2):
                for part in range(2):
                    relay_copy(kv, part).wait_send()

        for hh in range(together):
            @pl.when(climbs if hh == 0 else lev < levels - 2)
            def _():
                up_copy(1, me, hh).wait_send()

    @pl.when((col == 1) & climbs)
    def _():
        every(up_copy, 0, me, "wait_send")
        every(up_copy, 1, me, "wait_send")
        every(up_copy, 1, me - 1, "wait_send")
        for kv in range(2):
            for part in range(2):
                thru_copy(kv, part).wait_send()

    def sent(r, _):
        b = me - 2 * r
        every(side_copy, 0, b, "wait_send")

        @pl.when(climbs)
        def _():
            every(up_copy, 0, b, "wait_send")

            for hh in range(together):
                @pl.when((hh > 0) | (col == 1) | (r > 1) | (lev < levels - 2))
                def _():
                    up_copy(1, b, hh).wait_send()

        @pl.when(col == 1)
        def _():
            every(side_copy, 1, b, "wait_send")

            @pl.when(climbs)
            def _():
                every(up_copy, 1, b - 1, "wait_send")

            for hh in range(together):
                @pl.when((r == (2 if hh == 0 else 1)) & jnp.logical_not(climbs))
                def _():
                    side_copy(1, b - 1, hh).wait_send()
        return 0

    lax.fori_loop(1, lev + 1, sent, 0)


def shards(size, queries, keys, values):
    rows, heads, width = queries.shape
    own = rows // 8
    parts = 2 - heads % 2
    vmem = pl.BlockSpec(memory_space=pltpu.VMEM)
    return pl.pallas_call(
        functools.partial(kernel, size),
        out_shape=pltpu.VMEM((rows, heads, width), BF16),
        in_specs=[pl.BlockSpec(memory_space=pl.ANY)] * 3,
        out_specs=vmem,
        scratch_shapes=[
            pltpu.VMEM((rows, heads, width), BF16),
            pltpu.VMEM((rows, heads, width), BF16),
            pltpu.VMEM((rows, heads, width), BF16),
            pltpu.VMEM((2, parts, size, own, heads // parts, width), BF16),
            pltpu.VMEM((2, 2, BLOCK, heads, width), BF16),
            pltpu.VMEM((2, 2, BLOCK, heads, width), BF16),
            pltpu.VMEM((2, BLOCK, heads, width), BF16),
            pltpu.VMEM((heads, rows, width), BF16),
            pltpu.VMEM((2, heads, rows, width), BF16),
            pltpu.VMEM((2, heads, rows // 2 - BLOCK, width), BF16),
            pltpu.VMEM((2, heads, rows // 4 - BLOCK, width), BF16),
            pltpu.VMEM((2, heads, QUAD, width), BF16),
            pltpu.VMEM((2, heads, 4 * own, width), BF16),
            pltpu.VMEM((2, HALF, NEAR), F32),
            pltpu.VMEM((HALF, 3 * HALF), F32),
            pltpu.VMEM((QUAD, QUAD), F32),
            pltpu.VMEM((heads, rows, width), F32),
            pltpu.VMEM((heads, rows, width), F32),
            pltpu.VMEM((heads, rows, width), F32),
            pltpu.VMEM((80 * heads, width), F32),
            pltpu.VMEM((rows * heads, width), F32),
            pltpu.SemaphoreType.DMA((3,)),
            pltpu.SemaphoreType.DMA((2, parts, size)),
            pltpu.SemaphoreType.DMA((2, parts, size)),
            pltpu.SemaphoreType.DMA((2, parts, size)),
            pltpu.SemaphoreType.DMA((2, 2)),
            pltpu.SemaphoreType.DMA((2, 2)),
            pltpu.SemaphoreType.DMA((2, 2)),
            pltpu.SemaphoreType.DMA((2, 2)),
        ],
        compiler_params=pltpu.CompilerParams(
            collective_id=0, has_side_effects=True, vmem_limit_bytes=60 * 2**20),
    )(queries, keys, values)


def solution(mesh):
    spec = P(("groups", "seq"), "heads", None)
    return jax.shard_map(
        functools.partial(shards, mesh.shape["seq"]),
        mesh=mesh, in_specs=(spec,) * 3, out_specs=spec, check_vma=False)
```

```python
import functools
import math

import jax
import jax.numpy as jnp
from jax import lax
from jax.experimental import pallas as pl
from jax.experimental.pallas import tpu as pltpu
from jax.sharding import PartitionSpec as P

BLOCK = 64
QUAD = 4 * BLOCK
HALF = 2 * BLOCK
NEAR = 6 * BLOCK
NEG = -1e30
F32 = jnp.float32
BF16 = jnp.bfloat16


def to_heads(values, scratch, heads):
    count, _, width = values.shape
    scratch[pl.ds(0, count * heads), :] = values.reshape(count * heads, width)
    return [scratch[pl.ds(h, count, stride=heads), :].astype(BF16) for h in range(heads)]


def halved(values):
    count, heads, width = values.shape
    pairs = values.reshape(count // 2, 2, heads, width)
    return pairs[:, 0] + pairs[:, 1]


def across(column, count):
    width = column.shape[1]
    return jnp.concatenate([column] * (count // width), 1) if count > width else column


def with_ones(values):
    return jnp.concatenate([values, jnp.ones_like(values)], 1)


def kernel(size, q_hbm, k_hbm, v_hbm, o_ref,
           q_ref, k_ref, v_ref, far, tail, thru, sendp, eq, e0, e1, e2, before, fk,
           mask1, mask0, maskt, acc, top, total, tmp, otmp,
           in_sem, recv, up_send, side_send, t_send, t_recv, r_send, r_recv):
    rows, heads, width = q_ref.shape
    own = rows // 8
    blocks = rows // BLOCK
    gain = math.log2(math.e) / math.sqrt(width)
    me = lax.axis_index("seq")
    col = lax.rem(me, 2)
    lev = me // 2
    levels = size // 2
    together = 2 - heads % 2
    groups = heads // together
    early = (groups + 1) // 2
    share = heads // together
    climbs = lev < levels - 1
    pair = me + 1 - 2 * col
    up = jnp.minimum(me + 2, size - 1)
    sources = (k_ref, v_ref)

    def remote(src, dst, send, got, target):
        return pltpu.make_async_remote_copy(
            src_ref=src, dst_ref=dst, send_sem=send, recv_sem=got,
            device_id={"seq": target}, device_id_type=pl.DeviceIdType.MESH)

    def up_copy(kv, b, hh):
        place = far.at[kv, hh, b]
        return remote(place, place, up_send.at[kv, hh, b], recv.at[kv, hh, b], up)

    def side_copy(kv, b, hh):
        place = far.at[kv, hh, b]
        return remote(place, place, side_send.at[kv, hh, b], recv.at[kv, hh, b], pair)

    def every(copy, kv, b, action):
        for hh in range(together):
            getattr(copy(kv, b, hh), action)()

    def tail_source(kv, part):
        return sources[kv].at[pl.ds(rows - BLOCK, BLOCK)] if part == 0 else sendp.at[kv]

    def tail_copy(kv, part):
        return remote(tail_source(kv, part), tail.at[kv, part], t_send.at[kv, part], t_recv.at[kv, part], pair)

    def thru_copy(kv, part):
        return remote(tail_source(kv, part), thru.at[kv, part], t_send.at[kv, part], r_recv.at[kv, part], pair)

    def relay_copy(kv, part):
        return remote(thru.at[kv, part], tail.at[kv, part], r_send.at[kv, part], t_recv.at[kv, part], up)

    barrier = pltpu.get_barrier_semaphore()
    for step in (-2, 2):
        @pl.when((me + step >= 0) & (me + step < size))
        def _():
            pl.semaphore_signal(barrier, inc=1, device_id={"seq": me + step},
                                device_id_type=pl.DeviceIdType.MESH)
    pl.semaphore_signal(barrier, inc=1, device_id={"seq": pair}, device_id_type=pl.DeviceIdType.MESH)

    loads = [pltpu.make_async_copy(src, dst, in_sem.at[n]) for n, (src, dst) in enumerate(
        ((v_hbm, v_ref), (k_hbm, k_ref), (q_hbm, q_ref)))]
    for load in loads:
        load.start()

    def split(kv, c):
        x = sources[kv][pl.ds(c * BLOCK, BLOCK)].astype(F32)
        two = halved(x)
        four = halved(two)
        eight = halved(four)
        eight = (eight * 0.125).astype(BF16)
        for hh in range(together):
            far[kv, hh, me, pl.ds(c * 8, 8)] = eight[:, hh * share:(hh + 1) * share]
        if c == blocks - 2:
            sendp[kv, pl.ds(0, 32)] = (two * 0.5).astype(BF16)
        if blocks - 4 <= c < blocks - 2:
            sendp[kv, pl.ds(32 + 16 * (c - blocks + 4), 16)] = (four * 0.25).astype(BF16)

    def spread(kv, c):
        x = sources[kv][pl.ds(c * BLOCK, BLOCK)].astype(F32)
        for h, part in enumerate(to_heads(x, tmp, heads)):
            e0[kv, h, pl.ds(c * BLOCK, BLOCK), :] = part
        if c < blocks - 2:
            two = halved(x)
            for h, part in enumerate(to_heads(two * 0.5, tmp, heads)):
                e1[kv, h, pl.ds(c * 32, 32), :] = part
            if c < blocks - 4:
                four = halved(two)
                for h, part in enumerate(to_heads(four * 0.25, tmp, heads)):
                    e2[kv, h, pl.ds(c * 16, 16), :] = part

    for kv in (1, 0):
        loads[1 - kv].wait()
        for c in range(blocks):
            split(kv, c)

    pl.semaphore_wait(barrier, 1 + jnp.where(lev > 0, 1, 0) + jnp.where(climbs, 1, 0))

    @pl.when(col == 0)
    def _():
        every(side_copy, 1, me, "start")
        every(side_copy, 0, me, "start")

        @pl.when(climbs)
        def _():
            every(up_copy, 0, me, "start")

        for hh in range(together):
            @pl.when(climbs if hh == 0 else lev < levels - 2)
            def _():
                up_copy(1, me, hh).start()

    @pl.when((col == 1) & climbs)
    def _():
        every(up_copy, 0, me, "start")
        every(up_copy, 1, me, "start")
        for kv in range(2):
            for part in range(2):
                thru_copy(kv, part).start()

    for kv in range(2):
        for c in range(blocks):
            spread(kv, c)
    loads[2].wait()
    for c in range(blocks):
        x = q_ref[pl.ds(c * BLOCK, BLOCK)].astype(F32)
        for h, part in enumerate(to_heads(x, tmp, heads)):
            eq[h, pl.ds(c * BLOCK, BLOCK), :] = part

    def grid(count):
        return (lax.broadcasted_iota(jnp.int32, (HALF, count), 0),
                lax.broadcasted_iota(jnp.int32, (HALF, count), 1))

    i, j = grid(NEAR)
    level = jnp.where(j < 192, 0.0, jnp.where(j < 256, 1.0, jnp.where(j < 320, 2.0, 3.0)))
    seen01 = jnp.where(j < 192, jnp.where((j <= i + BLOCK) & ((j >= BLOCK) | (i < BLOCK)), 1, 0),
                       jnp.where((j < 224) | (i >= BLOCK), 1, 0))
    for hf in range(2):
        seen = jnp.where(j < 256, seen01, jnp.where(j < 320, jnp.where((j < 288) | (hf == 1), 1, 0), col))
        mask1[hf] = jnp.where(seen > 0, level, NEG)
    i, j = grid(HALF)
    mask0[:, pl.ds(0, HALF)] = jnp.where(j <= i, 0.0, NEG)
    i, j = grid(2 * HALF)
    seen0 = jnp.where(j < 192, jnp.where((j <= i + BLOCK) & ((j >= BLOCK) | (i < BLOCK)), 1, 0),
                      jnp.where((j < 224) | (i >= BLOCK), 1, 0))
    mask0[:, pl.ds(HALF, 2 * HALF)] = jnp.where(seen0 > 0, jnp.where(j < 192, 0.0, 1.0), NEG)
    ends = jnp.where(j < 192 + own // 2, col, 0)
    level = jnp.where(j < 64, 0.0, jnp.where(j < 128, 1.0, jnp.where(j < 192, 2.0, 3.0)))
    for hf in range(2):
        seent = jnp.where(j < 64, jnp.where(i < BLOCK, 1 - hf, 0),
                          jnp.where(j < 128, jnp.where((j < 96) | (i >= BLOCK), 1 - hf, 0),
                                    jnp.where(j < 192, jnp.where((j < 160) | (hf == 1), 1, 0), ends)))
        maskt[pl.ds(hf * HALF, HALF), :] = jnp.where(seent > 0, level, NEG)

    def begin(h, at, kk, vv, mask):
        s = lax.dot_general(eq[h, pl.ds(at, HALF), :], kk, (((1,), (1,)), ((), ())),
                            preferred_element_type=F32)
        s = s * gain + mask
        m = jnp.broadcast_to(jnp.max(s, axis=1, keepdims=True), (HALF, width))
        w = jnp.exp2(s - across(m, s.shape[1])).astype(BF16)
        both = jnp.dot(w, with_ones(vv), preferred_element_type=F32)
        top[h, pl.ds(at, HALF), :] = m
        acc[h, pl.ds(at, HALF), :] = both[:, :width]
        total[h, pl.ds(at, HALF), :] = both[:, width:]

    def near(qd, first, count):
        def body(g, _):
            for part in range(2 * share):
                h, hf = g * share + part // 2, part % 2
                at = qd * QUAD + hf * HALF
                kk, vv = (jnp.concatenate([
                    e0[kv, h, pl.ds(at - BLOCK, 192), :],
                    e1[kv, h, pl.ds(at // 2 - BLOCK, BLOCK), :],
                    e2[kv, h, pl.ds((qd - 1) * BLOCK, BLOCK), :],
                    before[kv, h, pl.ds(3 * BLOCK, BLOCK)]], 0) for kv in range(2))
                begin(h, at, kk, vv, mask1[hf])
            return 0
        lax.fori_loop(first, first + count, body, 0)

    def nearest(first, count):
        def body(g, _):
            for n in range(share):
                h = g * share + n
                begin(h, 0, e0[0, h, pl.ds(0, HALF), :], e0[1, h, pl.ds(0, HALF), :], mask0[:, pl.ds(0, HALF)])
                kk, vv = (jnp.concatenate([
                    e0[kv, h, pl.ds(BLOCK, 192), :], e1[kv, h, pl.ds(0, BLOCK), :]], 0) for kv in range(2))
                begin(h, HALF, kk, vv, mask0[:, pl.ds(HALF, 2 * HALF)])
            return 0
        lax.fori_loop(first, first + count, body, 0)

    def merge(h, at, count, s, vv, lift):
        m = top[h, pl.ds(at, count), :]
        peak = jnp.max(s, axis=1, keepdims=True)
        if lift is not None:
            peak = peak * gain + lift
            s = s * gain
        fresh = jnp.maximum(m, peak)
        fade = jnp.exp2(m - fresh)
        w = jnp.exp2(s - across(fresh if lift is None else fresh - lift, s.shape[1])).astype(BF16)
        both = jnp.dot(w, with_ones(vv), preferred_element_type=F32)
        top[h, pl.ds(at, count), :] = fresh
        acc[h, pl.ds(at, count), :] = acc[h, pl.ds(at, count), :] * fade + both[:, :width]
        total[h, pl.ds(at, count), :] = total[h, pl.ds(at, count), :] * fade + both[:, width:]

    def scores(h, at, count, kk):
        return lax.dot_general(eq[h, pl.ds(at, count), :], kk, (((1,), (1,)), ((), ())),
                               preferred_element_type=F32)

    def extra():
        @pl.when(col == 1)
        def _():
            every(side_copy, 0, me - 1, "wait_recv")
            for kv in range(2):
                for hh in range(together):
                    for h, part in enumerate(to_heads(far[kv, hh, me - 1].astype(F32), tmp, share)):
                        before[kv, hh * share + h, pl.ds(3 * BLOCK, own)] = part

        @pl.when(col == 0)
        def _():
            for kv in range(2):
                for h in range(heads):
                    before[kv, h, pl.ds(3 * BLOCK, own)] = jnp.zeros((own, width), BF16)

    def previous():
        for kv in range(2):
            for part in range(2):
                tail_copy(kv, part).wait_recv()
            x = tail[kv, 0].astype(F32)
            two = halved(x)
            four = halved(two)
            y = tail[kv, 1].astype(F32)
            late = halved(y[:32])
            for h, part in enumerate(to_heads(x, tmp, heads)):
                before[kv, h, pl.ds(0, BLOCK), :] = part
            for h, part in enumerate(to_heads(two * 0.5, tmp, heads)):
                before[kv, h, pl.ds(96, 32), :] = part
            for h, part in enumerate(to_heads(four * 0.25, tmp, heads)):
                before[kv, h, pl.ds(176, 16), :] = part
            for h, part in enumerate(to_heads(late * 0.5, tmp, heads)):
                before[kv, h, pl.ds(160, 16), :] = part
            for h, part in enumerate(to_heads(y, tmp, heads)):
                before[kv, h, pl.ds(64, 32), :] = part[:32]
                before[kv, h, pl.ds(128, 32), :] = part[32:]

        def body(g, _):
            for n in range(share):
                h = g * share + n
                s = scores(h, 0, QUAD, before[0, h]) * gain + maskt[...]
                merge(h, 0, QUAD, s, before[1, h], None)
            return 0
        lax.fori_loop(0, together, body, 0)

    def arrange(hh):
        for h in range(hh * share, (hh + 1) * share):
            for c in range(rows // HALF):
                otmp[pl.ds(c * HALF * heads + h, HALF, stride=heads), :] = (
                    acc[h, pl.ds(c * HALF, HALF), :] / total[h, pl.ds(c * HALF, HALF), :])

    def distant(lower, upper, final):
        place = lax.broadcasted_iota(jnp.int32, (1, 4 * own), 1)
        gone = (place >= 2 * own) & (upper == lower)
        inner = (col == 0) & (lower == 1) & (place >= own // 2) & (place < own)
        hides = [jnp.where(gone | inner, NEG, 0.0), jnp.where(gone, NEG, 0.0)]

        def fetch(r, hh, spot):
            odd = me - 2 * r + 1 - col
            even = me - 2 * r - col

            @pl.when((spot == 0) | (upper > lower))
            def _():
                @pl.when(col == 1)
                def _():
                    side_copy(0, even, hh).wait_recv()

                    @pl.when(r == 3)
                    def _():
                        up_copy(1, even, hh).wait_recv()

                        @pl.when(climbs)
                        def _():
                            up_copy(1, even, hh).start()

                    if hh > 0:
                        @pl.when((r == 2) & jnp.logical_not(climbs))
                        def _():
                            up_copy(1, even, hh).wait_recv()

                @pl.when(col == 0)
                def _():
                    side_copy(0, odd, hh).wait_recv()
                    side_copy(1, odd, hh).wait_recv()

                    @pl.when(jnp.logical_not(climbs))
                    def _():
                        side_copy(1, even, hh).wait_recv()
            for kv in range(2):
                for n, b in enumerate((odd, even)):
                    for h, part in enumerate(to_heads(far[kv, hh, b].astype(F32), tmp, share)):
                        fk[kv, hh * share + h, pl.ds((2 * spot + n) * own, own), :] = part

        def body(g, _):
            for n in range(share * (rows // QUAD)):
                h, qd = g * share + n // (rows // QUAD), n % (rows // QUAD)
                at = qd * QUAD
                s = scores(h, at, QUAD, fk[0, h]) + hides[min(qd, 1)]
                merge(h, at, QUAD, s, fk[1, h], 3.0)
            return 0

        for hh in range(together):
            fetch(lower, hh, 0)
            fetch(upper, hh, 1)
            lax.fori_loop(hh, hh + 1, body, 0)

            @pl.when(final)
            def _():
                arrange(hh)

    def climb(kv, b, side=None, halves=tuple(range(together))):
        for hh in halves:
            up_copy(kv, b, hh).wait_recv()

            @pl.when(climbs)
            def _():
                up_copy(kv, b, hh).start()
            if side is not None:
                side_copy(kv, b, hh).start()

    def odd_turn(n):
        def at(turn, r):
            return (n == turn) & (r <= lev)

        @pl.when(n == 1)
        def _():
            climb(1, me - 1)

        for turn, r in ((1, 1), (4, 2), (6, 3)):
            @pl.when(at(turn, r))
            def _():
                climb(0, me - 2 * r, True)

        for turn, r in ((2, 1), (5, 2), (6, 3)):
            @pl.when(at(turn, r))
            def _():
                climb(1, me - 2 * r, True)

        @pl.when(at(3, 1))
        def _():
            every(up_copy, 1, me - 3, "wait_recv")

            @pl.when(lev == levels - 1)
            def _():
                for hh in range(1, together):
                    side_copy(1, me - 3, hh).start()

            @pl.when(climbs)
            def _():
                up_copy(1, me - 3, 0).start()

            @pl.when(lev < levels - 2)
            def _():
                for hh in range(1, together):
                    up_copy(1, me - 3, hh).start()

        @pl.when(at(5, 2))
        def _():
            climb(1, me - 5, None, (0,))

            @pl.when(lev == levels - 1)
            def _():
                side_copy(1, me - 5, 0).start()

        @pl.when(at(5, 1) & (lev == levels - 2))
        def _():
            for hh in range(1, together):
                up_copy(1, me - 3, hh).start()

        @pl.when(at(5, 2) & climbs)
        def _():
            for hh in range(1, together):
                climb(1, me - 5, None, (hh,))

        @pl.when((n >= 8) & (n - 4 <= lev))
        def _():
            b = me - 2 * (n - 4)
            for kv in range(2):
                climb(kv, b, True)
            climb(1, b - 1)

    def even_turn(n):
        def relay(kv, part):
            @pl.when(climbs)
            def _():
                thru_copy(kv, part).wait_recv()
                relay_copy(kv, part).start()

        def cross(r):
            @pl.when(r <= lev)
            def _():
                climb(0, me - 2 * r, True)

        def rise(r):
            @pl.when((r <= lev) & climbs)
            def _():
                climb(1, me - 2 * r)

        @pl.when(n == 1)
        def _():
            cross(1)
            for kv in range(2):
                for part in range(2):
                    tail_copy(kv, part).start()
            relay(0, 0)

        @pl.when(n == 2)
        def _():
            relay(0, 1)

            @pl.when((lev >= 1) & climbs)
            def _():
                every(up_copy, 1, me - 2, "wait_recv")

                @pl.when(lev < levels - 2)
                def _():
                    every(up_copy, 1, me - 2, "start")

        @pl.when(n == 3)
        def _():
            cross(2)

        @pl.when(n == 4)
        def _():
            relay(1, 0)
            relay(1, 1)

            @pl.when((lev >= 2) & climbs)
            def _():
                climb(1, me - 4, None, (0,))

            @pl.when((lev >= 1) & (lev == levels - 2))
            def _():
                for hh in range(1, together):
                    up_copy(1, me - 2, hh).start()

            @pl.when((lev >= 2) & climbs)
            def _():
                for hh in range(1, together):
                    climb(1, me - 4, None, (hh,))

        @pl.when(n == 5)
        def _():
            cross(3)

        @pl.when(n == 7)
        def _():
            rise(3)

        @pl.when(n >= 8)
        def _():
            cross(n - 4)
            rise(n - 4)

    def turn(n, _):
        @pl.when(col == 1)
        def _():
            odd_turn(n)

        @pl.when(col == 0)
        def _():
            even_turn(n)

        first = lax.rem(n, 2)
        count = jnp.where(first < together, 1, 0)

        @pl.when(n < 2)
        def _():
            nearest(first, count)

        @pl.when(n == 2)
        def _():
            extra()

        @pl.when((n == 2) | (n == 3))
        def _():
            for qd in range(1, rows // QUAD):
                near(qd, first, count)

        @pl.when((n == jnp.where(lev == 2, 5, 6)) & (me > 0))
        def _():
            previous()

        upper = jnp.where(n < 6, n - 3, n - 4)
        lower = jnp.maximum(upper - 1, 1)
        even = lax.rem(lev - upper, 2) == 0

        @pl.when((n >= 4) & (n != 6) & (upper <= lev) & even)
        def _():
            distant(lower, upper, (n >= 7) & (upper == lev))
        return 0

    lax.fori_loop(0, jnp.maximum(6, lev + 4) + 1, turn, 0)

    @pl.when(lev < 3)
    def _():
        for hh in range(together):
            arrange(hh)

    for c in range(rows // HALF):
        o_ref[pl.ds(c * HALF, HALF)] = (
            otmp[pl.ds(c * HALF * heads, HALF * heads), :].reshape(HALF, heads, width).astype(BF16))

    @pl.when(col == 0)
    def _():
        every(side_copy, 1, me, "wait_send")
        every(side_copy, 0, me, "wait_send")
        for kv in range(2):
            for part in range(2):
                tail_copy(kv, part).wait_send()

        @pl.when(climbs)
        def _():
            every(up_copy, 0, me, "wait_send")
            for kv in range(2):
                for part in range(2):
                    relay_copy(kv, part).wait_send()

        for hh in range(together):
            @pl.when(climbs if hh == 0 else lev < levels - 2)
            def _():
                up_copy(1, me, hh).wait_send()

    @pl.when((col == 1) & climbs)
    def _():
        every(up_copy, 0, me, "wait_send")
        every(up_copy, 1, me, "wait_send")
        every(up_copy, 1, me - 1, "wait_send")
        for kv in range(2):
            for part in range(2):
                thru_copy(kv, part).wait_send()

    def sent(r, _):
        b = me - 2 * r
        every(side_copy, 0, b, "wait_send")

        @pl.when(climbs)
        def _():
            every(up_copy, 0, b, "wait_send")

            for hh in range(together):
                @pl.when((hh > 0) | (col == 1) | (r > 1) | (lev < levels - 2))
                def _():
                    up_copy(1, b, hh).wait_send()

        @pl.when(col == 1)
        def _():
            every(side_copy, 1, b, "wait_send")

            @pl.when(climbs)
            def _():
                every(up_copy, 1, b - 1, "wait_send")

            for hh in range(together):
                @pl.when((r == (2 if hh == 0 else 1)) & jnp.logical_not(climbs))
                def _():
                    side_copy(1, b - 1, hh).wait_send()
        return 0

    lax.fori_loop(1, lev + 1, sent, 0)


def shards(size, queries, keys, values):
    rows, heads, width = queries.shape
    own = rows // 8
    parts = 2 - heads % 2
    vmem = pl.BlockSpec(memory_space=pltpu.VMEM)
    return pl.pallas_call(
        functools.partial(kernel, size),
        out_shape=pltpu.VMEM((rows, heads, width), BF16),
        in_specs=[pl.BlockSpec(memory_space=pl.ANY)] * 3,
        out_specs=vmem,
        scratch_shapes=[
            pltpu.VMEM((rows, heads, width), BF16),
            pltpu.VMEM((rows, heads, width), BF16),
            pltpu.VMEM((rows, heads, width), BF16),
            pltpu.VMEM((2, parts, size, own, heads // parts, width), BF16),
            pltpu.VMEM((2, 2, BLOCK, heads, width), BF16),
            pltpu.VMEM((2, 2, BLOCK, heads, width), BF16),
            pltpu.VMEM((2, BLOCK, heads, width), BF16),
            pltpu.VMEM((heads, rows, width), BF16),
            pltpu.VMEM((2, heads, rows, width), BF16),
            pltpu.VMEM((2, heads, rows // 2 - BLOCK, width), BF16),
            pltpu.VMEM((2, heads, rows // 4 - BLOCK, width), BF16),
            pltpu.VMEM((2, heads, QUAD, width), BF16),
            pltpu.VMEM((2, heads, 4 * own, width), BF16),
            pltpu.VMEM((2, HALF, NEAR), F32),
            pltpu.VMEM((HALF, 3 * HALF), F32),
            pltpu.VMEM((QUAD, QUAD), F32),
            pltpu.VMEM((heads, rows, width), F32),
            pltpu.VMEM((heads, rows, width), F32),
            pltpu.VMEM((heads, rows, width), F32),
            pltpu.VMEM((80 * heads, width), F32),
            pltpu.VMEM((rows * heads, width), F32),
            pltpu.SemaphoreType.DMA((3,)),
            pltpu.SemaphoreType.DMA((2, parts, size)),
            pltpu.SemaphoreType.DMA((2, parts, size)),
            pltpu.SemaphoreType.DMA((2, parts, size)),
            pltpu.SemaphoreType.DMA((2, 2)),
            pltpu.SemaphoreType.DMA((2, 2)),
            pltpu.SemaphoreType.DMA((2, 2)),
            pltpu.SemaphoreType.DMA((2, 2)),
        ],
        compiler_params=pltpu.CompilerParams(
            collective_id=0, has_side_effects=True, vmem_limit_bytes=60 * 2**20),
    )(queries, keys, values)


def solution(mesh):
    spec = P(("groups", "seq"), "heads", None)
    return jax.shard_map(
        functools.partial(shards, mesh.shape["seq"]),
        mesh=mesh, in_specs=(spec,) * 3, out_specs=spec, check_vma=False)
```
